256 devices in a mesh: ctx: 32 (over y, x, core), head: 4 (over z_lo), dp: 2 (over z_hi).
Axes of the slice: x: 4, y: 4, z: 8 (z_hi: 2, z_lo: 4; z = z_hi * 4 + z_lo), core: 2. Of those that a mesh axis runs over, the one named last changes fastest.
Arguments:
- queries: bfloat16 [2, 8192, 4096], P('dp', 'ctx', 'head'), may hold values from -6 to 6
- keys: bfloat16 [2, 8192, 4096], P('dp', 'ctx', 'head'), may hold values from -6 to 6
- values: bfloat16 [2, 8192, 4096], P('dp', 'ctx', 'head'), may hold values from -6 to 6
- log_decay: float32 [2, 32, 8192], P('dp', 'head', 'ctx'), may hold values from -1.5 to 0
- w_out: bfloat16 [128, 32, 3072], P(('ctx', 'dp'), 'head'), may hold values from -0.09375 to 0.09375
- grad_out: bfloat16 [2, 8192, 3072], P('dp', 'ctx'), may hold values from -6 to 6
Outputs:
- mixed: bfloat16 [2, 8192, 3072], P('dp', 'ctx', 'head')
- query_grad: bfloat16 [2, 8192, 4096], P('dp', 'ctx', 'head')
- key_grad: bfloat16 [2, 8192, 4096], P('dp', 'ctx', 'head')
- value_grad: bfloat16 [2, 8192, 4096], P('dp', 'ctx', 'head')
- w_grad: float32 [128, 32, 3072], P(('ctx', 'dp'), 'head')
The draws below stay inside these ranges and needn't reach their ends.
All inputs are finite; a program needn't handle non-finite values.
Results may differ from the reference program's by a relative error of at most 0.015.
Values may be sent and summed in bfloat16 or wider, within the bound.
A program may use at most 128 MiB of HBM per device.

```python
import jax
import jax.numpy as jnp
from jax import lax

H = 32
DH = 128
DOUT = 3072
BLOCK = 256
LENGTH = 8192
SEQS = 2


def draw_log_decay(key, part):
    streams = jax.random.split(key, 7)
    slow_count = 4
    slow = jax.random.randint(streams[0], (SEQS, H, 1, 1), 0, 8) < slow_count
    quick_decay_rate = jnp.exp(jax.random.uniform(streams[1], (SEQS, H, 1, 1), jnp.float32, jnp.log(1.0 / 50.0), jnp.log(1.0 / 30.0)))
    slow_rate = jnp.exp(jax.random.uniform(streams[2], (SEQS, H, 1, 1), jnp.float32, jnp.log(0.05 / LENGTH), jnp.log(0.5 / LENGTH)))
    base = jnp.where(slow, slow_rate, quick_decay_rate)
    block_total = LENGTH // BLOCK
    tile_shrinkage = jnp.exp(jax.random.uniform(streams[3], (SEQS, H, block_total, 1), jnp.float32, jnp.log(0.5), jnp.log(2.0)))
    place_factor = jnp.exp(jax.random.uniform(streams[4], (SEQS, H, block_total, BLOCK), jnp.float32, jnp.log(0.5), jnp.log(2.0)))
    fading_speed = (base * tile_shrinkage * place_factor).reshape(SEQS, H, LENGTH)
    spots = jax.random.randint(streams[5], (SEQS, H, 3, 1), 0, LENGTH)
    learning_loss = jax.random.uniform(streams[6], (SEQS, H, 3, 1), jnp.float32, 0.2, 0.35)
    agreeing_tally = spots == jnp.arange(LENGTH)[None, None, None, :]
    packet_batches = jnp.sum(jnp.where(agreeing_tally, jnp.log(1.0 - learning_loss), 0.0), axis=2)
    return (packet_batches - fading_speed).astype(jnp.float32)


def levels(rng, extent, cuts, smallest, largest):
    def one(dim, parts):
        steps = jax.random.uniform(jax.random.fold_in(jax.random.fold_in(rng, 6), dim), (parts,), jnp.float32, smallest / len(cuts), largest / len(cuts))
        return jnp.repeat(jnp.exp(steps), extent[dim] // parts).reshape((-1,) + (1,) * (len(extent) - dim - 1))

    gain = one(*cuts[0])
    for cut in cuts[1:]:
        gain = gain * one(*cut)
    return gain


def noise(key, shape, deviation, reach, pieces=(), held_as=jnp.bfloat16):
    values = deviation * jax.random.normal(key, shape, jnp.float32)
    if pieces:
        values = values * levels(key, shape, pieces, -0.22, 0.18)
    return jnp.clip(values, -reach, reach).astype(held_as)


def setup_inputs(seed: int = 0) -> dict:
    seeds = jax.random.split(jax.random.key(seed), 7)
    queries = noise(seeds[0], (SEQS, LENGTH, H * DH), 1.0, 6.0, ((0, 2), (1, 32), (2, 4)))
    keys = noise(seeds[1], (SEQS, LENGTH, H * DH), 1.0, 6.0, ((0, 2), (1, 32), (2, 4)))
    values = noise(seeds[2], (SEQS, LENGTH, H * DH), 1.0, 6.0, ((0, 2), (1, 32), (2, 4)))
    log_decay = draw_log_decay(jax.random.fold_in(seeds[6], 71), 0)
    w_out = noise(seeds[4], (DH, H, DOUT), (H * DH) ** -0.5, 0.09375, ((0, 64), (1, 4)))
    grad_out = noise(seeds[5], (SEQS, LENGTH, DOUT), 1.0, 6.0, ((0, 2), (1, 32)))
    return dict(queries=queries, keys=keys, values=values, log_decay=log_decay, w_out=w_out, grad_out=grad_out)


def block_weights(cumul):
    width = cumul.shape[-1]
    places = jnp.arange(width)
    lower = places[:, None] >= places[None, :]
    spread = cumul[..., :, None] - cumul[..., None, :]
    return jnp.exp(jnp.where(lower, spread, -jnp.inf))


def to_blocks(array, block_total):
    return array.reshape(block_total, BLOCK, H, DH).transpose(0, 2, 1, 3)


def from_blocks(array, block_total):
    return array.transpose(0, 2, 1, 3).reshape(block_total * BLOCK, H * DH)


def reference(queries, keys, values, log_decay, w_out, grad_out):
    scale = 1.0 / DH
    block_total = LENGTH // BLOCK
    panel = w_out.astype(jnp.float32)
    w_grad = jnp.zeros((DH, H, DOUT), jnp.float32)
    mixed_list = []
    qgrad_list = []
    kgrad_list = []
    vgrad_list = []
    for sequence in range(SEQS):
        query_blocks = to_blocks(queries[sequence], block_total)
        key_blocks = to_blocks(keys[sequence], block_total)
        value_blocks = to_blocks(values[sequence], block_total)
        cumul = jnp.cumsum(log_decay[sequence].reshape(H, block_total, BLOCK).transpose(1, 0, 2), axis=-1)

        def forward_step(state, inputs):
            query_here, key_here, value_here, cumul_here = inputs
            weights = block_weights(cumul_here)
            scores = jnp.einsum('htd,hjd->htj', query_here.astype(jnp.float32), key_here.astype(jnp.float32))
            probs = (scores * scale * weights).astype(jnp.bfloat16)
            state_low = state.astype(jnp.bfloat16)
            decay_multiplier = scale * jnp.exp(cumul_here)
            intra = jnp.einsum('htj,hjd->htd', probs.astype(jnp.float32), value_here.astype(jnp.float32))
            inter = jnp.einsum('htd,hde->hte', query_here.astype(jnp.float32), state_low.astype(jnp.float32))
            attended = (intra + inter * decay_multiplier[:, :, None]).astype(jnp.bfloat16)
            tail = jnp.exp(cumul_here[:, -1:] - cumul_here)
            keys_weighted = (key_here.astype(jnp.float32) * tail[:, :, None]).astype(jnp.bfloat16)
            contrib = jnp.einsum('htd,hte->hde', keys_weighted.astype(jnp.float32), value_here.astype(jnp.float32))
            new_state = jnp.exp(cumul_here[:, -1])[:, None, None] * state + contrib
            return new_state, (attended, state_low)

        start_state = jnp.zeros((H, DH, DH), jnp.float32)
        _, (attended_blocks, state_blocks) = lax.scan(forward_step, start_state, (query_blocks, key_blocks, value_blocks, cumul))
        attended_row_list = from_blocks(attended_blocks, block_total).reshape(LENGTH, H, DH)
        cotangent = grad_out[sequence].astype(jnp.float32)
        mixed = jnp.einsum('thd,dho->to', attended_row_list.astype(jnp.float32), panel).astype(jnp.bfloat16)
        grad_heads = jnp.einsum('to,dho->thd', cotangent, panel).astype(jnp.bfloat16)
        w_grad = w_grad + jnp.einsum('thd,to->dho', attended_row_list.astype(jnp.float32), cotangent)
        grad_blocks = to_blocks(grad_heads.reshape(LENGTH, H * DH), block_total)

        def backward_step(back_state, inputs):
            query_here, key_here, value_here, grad_here, cumul_here, state_low = inputs
            weights = block_weights(cumul_here)
            query_f = query_here.astype(jnp.float32)
            key_f = key_here.astype(jnp.float32)
            value_f = value_here.astype(jnp.float32)
            grad_f = grad_here.astype(jnp.float32)
            scores = jnp.einsum('htd,hjd->htj', query_f, key_f)
            probs = (scores * scale * weights).astype(jnp.bfloat16)
            logit_gradient = jnp.einsum('hte,hje->htj', grad_f, value_f)
            dprobs = (logit_gradient * scale * weights).astype(jnp.bfloat16)
            back_low = back_state.astype(jnp.bfloat16)
            decay_multiplier = scale * jnp.exp(cumul_here)
            tail = jnp.exp(cumul_here[:, -1:] - cumul_here)
            dprobs_f = dprobs.astype(jnp.float32)
            back_f = back_low.astype(jnp.float32)
            query_grad = jnp.einsum('htj,hjd->htd', dprobs_f, key_f) + jnp.einsum('hte,hde->htd', grad_f, state_low.astype(jnp.float32)) * decay_multiplier[:, :, None]
            key_grad = jnp.einsum('htj,htd->hjd', dprobs_f, query_f) + tail[:, :, None] * jnp.einsum('hje,hde->hjd', value_f, back_f)
            value_grad = jnp.einsum('htj,hte->hje', probs.astype(jnp.float32), grad_f) + tail[:, :, None] * jnp.einsum('hjd,hde->hje', key_f, back_f)
            queries_weighted = (query_f * decay_multiplier[:, :, None]).astype(jnp.bfloat16)
            earlier = jnp.exp(cumul_here[:, -1])[:, None, None] * back_state + jnp.einsum('htd,hte->hde', queries_weighted.astype(jnp.float32), grad_f)
            return earlier, (query_grad.astype(jnp.bfloat16), key_grad.astype(jnp.bfloat16), value_grad.astype(jnp.bfloat16))

        end_state = jnp.zeros((H, DH, DH), jnp.float32)
        _, (qgrad_blocks, kgrad_blocks, vgrad_blocks) = lax.scan(backward_step, end_state, (query_blocks, key_blocks, value_blocks, grad_blocks, cumul, state_blocks), reverse=True)
        mixed_list.append(mixed)
        qgrad_list.append(from_blocks(qgrad_blocks, block_total))
        kgrad_list.append(from_blocks(kgrad_blocks, block_total))
        vgrad_list.append(from_blocks(vgrad_blocks, block_total))
    return (jnp.stack(mixed_list), jnp.stack(qgrad_list), jnp.stack(kgrad_list), jnp.stack(vgrad_list), w_grad)
```

```python
import jax
import jax.numpy as jnp
from jax import lax
from jax.experimental import pallas as pl
from jax.experimental.pallas import tpu as pltpu
from jax.sharding import PartitionSpec as P

DH = 128
BLOCK = 256
HEADS = 8
DOUT = 3072
HALF = DOUT // 2
CTX = 32
SCALE = 1.0 / DH
F32 = jnp.float32
BF16 = jnp.bfloat16
NT = (((1,), (1,)), ((), ()))
NN = (((1,), (0,)), ((), ()))
TN = (((0,), (0,)), ((), ()))


def mm(a, b, dims):
    return lax.dot_general(a, b, dims, preferred_element_type=F32)


class Ids:
    def __init__(self):
        self.names = {}

    def __call__(self, *name):
        return self.names.setdefault(name, len(self.names))


def kernel(
    q_ref, k_ref, v_ref, ld_ref, w_ref, go_ref,
    mixed_ref, qg_ref, kg_ref, vg_ref, wg_ref,
    panel, pt, cum, ccol, probs, intra, kpart, vpart, att, attp, gh,
    cf, rf, ef, low, cb, rb, eb, back,
    go_sib, att_t, att_sib,
    wp, wacc, xb, yb, wa, xa, ya, xz,
    mp, macc, mr1, mr2,
    ssem, rsem, a2a_s, a2a_r,
):
    ctx, head, dp = lax.axis_index("ctx"), lax.axis_index("head"), lax.axis_index("dp")
    core = ctx % 2
    x, y = (ctx // 2) % 4, ctx // 8
    a = x * (1 - core) + y * core
    b = y * (1 - core) + x * core
    ap, am, ao = (a + 1) % 4, (a + 3) % 4, (a + 2) % 4
    bp, bm, bo = (b + 1) % 4, (b + 3) % 4, (b + 2) % 4
    z, zo = dp, 1 - dp

    def at(a1, b1):
        x1 = a1 * (1 - core) + b1 * core
        y1 = b1 * (1 - core) + a1 * core
        return ((y1 * 4 + x1) * 2 + core, head, dp)

    dev_ap, dev_am, dev_bp, dev_bm = at(ap, b), at(am, b), at(a, bp), at(a, bm)
    dev_sib = (ctx + 1 - 2 * core, head, dp)
    dev_z = (ctx, head, zo)
    h1 = head + 1 - 2 * (head % 2)
    h2 = (head + 2) % 4
    h3 = (h1 + 2) % 4
    dev_h1, dev_h2 = (ctx, h1, dp), (ctx, h2, dp)

    ids = Ids()
    started = []

    def xfer(name, src, dst, dev):
        i = ids(*name)
        return pltpu.make_async_remote_copy(
            src_ref=src, dst_ref=dst, send_sem=ssem.at[i], recv_sem=rsem.at[i],
            device_id=dev, device_id_type=pl.DeviceIdType.MESH,
        )

    def send(name, src, dst, dev):
        copy = xfer(name, src, dst, dev)
        copy.start()
        started.append(copy)

    def recv(name, ref, dev):
        xfer(name, ref, ref, dev).wait_recv()

    barrier = pltpu.get_barrier_semaphore()

    def greet(i, carry):
        pl.semaphore_signal(
            barrier, inc=1, device_id=((ctx + i) % CTX, head, dp), device_id_type=pl.DeviceIdType.MESH
        )
        return carry

    lax.fori_loop(1, CTX, greet, 0)
    for dev in (dev_z, dev_h1, dev_h2):
        pl.semaphore_signal(barrier, inc=1, device_id=dev, device_id_type=pl.DeviceIdType.MESH)
    pl.semaphore_wait(barrier, CTX - 1 + 3)

    def slot(a1, b1, z1):
        return core * 32 + b1 * 8 + a1 * 2 + z1

    def whole(s):
        return panel.at[s]

    def part(s, h):
        return panel.at[s, :, pl.ds(h * HALF, HALF)]

    a_of = {0: a, 1: am, 2: ap, 3: ao}

    def b_sends(zi, k):
        zz = (z, zo)[zi]
        ref = whole(slot(a_of[k], b, zz))
        send(("bp", zi, k), ref, ref, dev_bp)
        send(("bm", zi, k), ref, ref, dev_bm)

    def a_sends(zi):
        ref = whole(slot(a, b, (z, zo)[zi]))
        send(("ap", zi), ref, ref, dev_ap)
        send(("am", zi), ref, ref, dev_am)

    def step_a(zi):
        zz = (z, zo)[zi]
        left, right = slot(am, b, zz), slot(ap, b, zz)
        recv(("ap", zi), whole(left), dev_am)
        send(("afp", zi), part(left, 0), part(left, 0), dev_ap)
        b_sends(zi, 1)
        recv(("am", zi), whole(right), dev_ap)
        send(("afm", zi), part(right, 1), part(right, 1), dev_am)
        b_sends(zi, 2)

    def step_ao(zi):
        far = slot(ao, b, (z, zo)[zi])
        recv(("afp", zi), part(far, 0), dev_am)
        recv(("afm", zi), part(far, 1), dev_ap)
        b_sends(zi, 3)

    def step_b(zi, k):
        zz = (z, zo)[zi]
        below, above = slot(a_of[k], bm, zz), slot(a_of[k], bp, zz)
        recv(("bp", zi, k), whole(below), dev_bm)
        send(("bfp", zi, k), part(below, 0), part(below, 0), dev_bp)
        recv(("bm", zi, k), whole(above), dev_bp)
        send(("bfm", zi, k), part(above, 1), part(above, 1), dev_bm)

    def step_bo(zi, k):
        far = slot(a_of[k], bo, (z, zo)[zi])
        recv(("bfp", zi, k), part(far, 0), dev_bm)
        recv(("bfm", zi, k), part(far, 1), dev_bp)

    def step_z():
        recv(("z",), whole(slot(a, b, zo)), dev_z)
        a_sends(1)
        b_sends(1, 0)

    def row(c1, b1):
        return panel.at[pl.ds(c1 * 32 + b1 * 8, 8)]

    def sib_send(k):
        ref = row(core, (b, bm, bp, bo)[k])
        send(("sib", k), ref, ref, dev_sib)

    def sib_recv(k):
        recv(("sib", k), row(1 - core, (a, am, ap, ao)[k]), dev_sib)

    mine = slot(a, b, z)
    panel[mine] = w_ref[...]
    send(("z",), whole(mine), whole(mine), dev_z)
    a_sends(0)
    b_sends(0, 0)
    send(("go",), go_ref, go_sib, dev_sib)

    t_row = lax.broadcasted_iota(jnp.int32, (BLOCK, BLOCK), 0)
    t_col = lax.broadcasted_iota(jnp.int32, (BLOCK, BLOCK), 1)
    upper = (t_row <= t_col).astype(F32)
    cum[...] = jnp.dot(ld_ref[...], upper, precision=lax.Precision.HIGHEST, preferred_element_type=F32)

    def lanes(h):
        return pl.ds(pl.multiple_of(h * DH, DH), DH)

    def weights(h):
        col = ccol[h]
        spread = jnp.concatenate([col, col], axis=1) - cum[pl.ds(h, 1), :]
        rows = lax.broadcasted_iota(jnp.int32, (BLOCK, BLOCK), 0)
        cols = lax.broadcasted_iota(jnp.int32, (BLOCK, BLOCK), 1)
        return jnp.exp(jnp.where(rows >= cols, spread, -jnp.inf))

    def pieces(buf, h, total, decay):
        for r in range(4):
            buf[h * 4 + r, 0:32, :] = total[r * 32 : (r + 1) * 32]
            buf[h * 4 + r, 32:40, :] = jnp.broadcast_to(decay, (8, DH))

    def fwd_share(h, carry):
        wide = jnp.broadcast_to(cum[pl.ds(h, 1), :], (DH, BLOCK))
        col = wide.T
        ccol[h] = col
        last = col[BLOCK - 1 : BLOCK, :]
        kw = (k_ref[:, lanes(h)].astype(F32) * jnp.exp(last - col)).astype(BF16)
        pieces(cf, h, mm(kw, v_ref[:, lanes(h)], TN), jnp.exp(last))
        return carry

    lax.fori_loop(0, HEADS, fwd_share, 0)

    def a2a(n, src, dst, i, out):
        other = (ctx + i) % CTX if out else (ctx + CTX - i) % CTX
        return pltpu.make_async_remote_copy(
            src_ref=src.at[other], dst_ref=dst.at[ctx if out else other],
            send_sem=a2a_s.at[n, i], recv_sem=a2a_r.at[n, i],
            device_id=(other, head, dp), device_id_type=pl.DeviceIdType.MESH,
        )

    def a2a_start(n, src, dst):
        def go(i, carry):
            a2a(n, src, dst, i, True).start()
            return carry

        lax.fori_loop(1, CTX, go, 0)
        dst[ctx] = src[ctx]

    def a2a_recv(n, src, dst):
        def go(i, carry):
            a2a(n, src, dst, i, False).wait_recv()
            return carry

        lax.fori_loop(1, CTX, go, 0)

    def a2a_sent(n, src, dst):
        def go(i, carry):
            a2a(n, src, dst, i, True).wait_send()
            return carry

        lax.fori_loop(1, CTX, go, 0)

    def scan(got, out, reverse):
        def go(i, state):
            at_block = CTX - 1 - i if reverse else i
            out[at_block] = state.astype(BF16)
            return state * got[at_block, 32:33, :] + got[at_block, 0:32, :]

        lax.fori_loop(0, CTX, go, jnp.zeros((32, DH), F32))

    def state_of(buf, h):
        return buf[pl.ds(h * 4, 4)].reshape(DH, DH)

    a2a_start(0, cf, rf)
    step_a(0)
    step_z()

    def inside(h, carry):
        scores = mm(q_ref[:, lanes(h)], k_ref[:, lanes(h)], NT)
        p = (scores * SCALE * weights(h)).astype(BF16)
        probs[h] = p
        intra[:, lanes(h)] = mm(p, v_ref[:, lanes(h)], NN)
        return carry

    lax.fori_loop(0, HEADS // 2, inside, 0)
    step_ao(0)
    step_b(0, 0)
    step_a(1)
    lax.fori_loop(HEADS // 2, HEADS, inside, 0)
    a2a_recv(0, cf, rf)
    scan(rf, ef, False)
    a2a_start(1, ef, low)
    step_b(0, 1)
    step_b(0, 2)
    step_ao(1)
    step_b(1, 0)
    sib_send(0)

    r = lax.broadcasted_iota(jnp.int32, (1024, DH), 0)
    place = r >> 4
    pc, pb, pa, pz = place >> 5, (place >> 3) & 3, (place >> 1) & 3, place & 1
    px = jnp.where(pc == 0, pa, pb)
    py = jnp.where(pc == 0, pb, pa)
    feature = 2 * ((((py * 4) + px) * 2 + pc) * 2 + pz) + ((r >> 3) & 1)
    lane = lax.broadcasted_iota(jnp.int32, (1024, DH), 1)
    same = feature == lane
    for h in range(HEADS):
        pt[:, h * DH : (h + 1) * DH] = jnp.where(same & ((r & 7) == h), 1.0, 0.0).astype(BF16)

    step_b(0, 3)
    step_b(1, 1)
    step_b(1, 2)

    a2a_recv(1, ef, low)

    def attend(h, carry):
        inter = mm(q_ref[:, lanes(h)], state_of(low, h), NN)
        factor = SCALE * jnp.exp(ccol[h])
        att[:, lanes(h)] = (intra[:, lanes(h)] + inter * factor).astype(BF16)
        return carry

    lax.fori_loop(0, HEADS, attend, 0)
    step_b(1, 3)
    sib_send(1)
    sib_send(2)

    def turn(i, carry):
        rows = pl.ds(pl.multiple_of(i * 256, 256), 256)
        att_t[rows, :] = mm(pt[rows, :], att[...], NT).astype(BF16)
        attp[:, rows] = mm(att[...], pt[rows, :], NT).astype(BF16)
        return carry

    lax.fori_loop(0, 4, turn, 0)
    other_rows = pl.ds(pl.multiple_of((1 - core) * 512, 512), 512)
    send(("att",), att_t.at[other_rows], att_sib, dev_sib)
    for zi in range(2):
        for k in range(4):
            step_bo(zi, k)
    sib_send(3)

    for k in range(4):
        sib_recv(k)

    def heads_grad(i, carry):
        rows = panel[pl.ds(i * 16, 16)].reshape(256, DOUT)
        attp_cols = pl.ds(pl.multiple_of(i * 256, 256), 256)
        gh[:, attp_cols] = mm(go_ref[...], rows, NT).astype(BF16)
        return carry

    lax.fori_loop(0, 4, heads_grad, 0)
    by_head = []
    for n in range(4):
        by_head.append(mm(gh[...], pt[:, n * 256 : (n + 1) * 256], NN).astype(BF16))
    for n in range(4):
        gh[:, n * 256 : (n + 1) * 256] = by_head[n]

    def bwd_share(h, carry):
        qw = (q_ref[:, lanes(h)].astype(F32) * (SCALE * jnp.exp(ccol[h]))).astype(BF16)
        last = ccol[h, BLOCK - 1 : BLOCK, :]
        pieces(cb, h, mm(qw, gh[:, lanes(h)], TN), jnp.exp(last))
        return carry

    lax.fori_loop(0, HEADS, bwd_share, 0)
    a2a_start(2, cb, rb)

    def mix(dest, store):
        def go(n, carry):
            cols = pl.ds(pl.multiple_of(dest * 768 + n * 256, 256), 256)
            w = panel[:, :, cols].reshape(1024, 256)
            store(pl.ds(pl.multiple_of(n * 256, 256), 256), mm(attp[...], w, NN))
            return carry

        lax.fori_loop(0, 3, go, 0)

    def store_at(dest):
        def store(cols, value):
            mp[dest, :, cols] = value.astype(BF16)

        return store

    def store_own(cols, value):
        macc[:, cols] = value

    mix(h3, store_at(h3))
    send(("m", 0), mp.at[h3], mr1.at[0], dev_h1)
    mix(h1, store_at(h1))
    send(("m", 1), mp.at[h1], mr1.at[1], dev_h1)

    recv(("go",), go_sib, dev_sib)
    recv(("att",), att_sib, dev_sib)

    def w_rows(b1, n):
        cols = pl.ds(pl.multiple_of(n * 256, 256), 256)
        own = att_t[pl.ds(pl.multiple_of(core * 512 + b1 * 128, 128), 128), :]
        sib = att_sib[pl.ds(pl.multiple_of(b1 * 128, 128), 128), :]
        return cols, mm(own, go_ref[:, cols], NN) + mm(sib, go_sib[:, cols], NN)

    def w_block(b1):
        def go(n, carry):
            cols, value = w_rows(b1, n)
            wp[b1, :, cols] = value.astype(BF16)
            return carry

        lax.fori_loop(0, 12, go, 0)

    def w_own(n, carry):
        cols, value = w_rows(b, n)
        wacc[:, cols] = value
        return carry

    lo, hi = pl.ds(0, HALF), pl.ds(HALF, HALF)
    w_block(bo)
    send(("w", 0), wp.at[bo, :, lo], xb.at[0], dev_bp)
    send(("w", 1), wp.at[bo, :, hi], xb.at[1], dev_bm)
    w_block(bp)
    send(("w", 2), wp.at[bp, :, hi], yb.at[0, :, hi], dev_bp)
    w_block(bm)
    send(("w", 3), wp.at[bm, :, lo], yb.at[1, :, lo], dev_bm)
    lax.fori_loop(0, 12, w_own, 0)
    mix(h2, store_at(h2))
    mix(head, store_own)

    def grads(h, carry):
        g, kk, vv, qq = gh[:, lanes(h)], k_ref[:, lanes(h)], v_ref[:, lanes(h)], q_ref[:, lanes(h)]
        dp_h = (mm(g, vv, NT) * SCALE * weights(h)).astype(BF16)
        factor = SCALE * jnp.exp(ccol[h])
        qg = mm(dp_h, kk, NN) + mm(g, state_of(low, h), NT) * factor
        qg_ref[:, lanes(h)] = qg.astype(BF16)
        kpart[:, lanes(h)] = mm(dp_h, qq, TN)
        vpart[:, lanes(h)] = mm(probs[h], g, TN)
        return carry

    def widen(ref):
        return ref.astype(F32)

    lax.fori_loop(0, 2, grads, 0)
    a2a_recv(2, cb, rb)
    scan(rb, eb, True)
    a2a_start(3, eb, back)

    recv(("w", 0), xb.at[0], dev_bm)
    wp[bp, :, lo] = (widen(wp[bp, :, lo]) + widen(xb[0])).astype(BF16)
    send(("w", 4), wp.at[bp, :, lo], yb.at[0, :, lo], dev_bp)
    recv(("w", 1), xb.at[1], dev_bp)
    wp[bm, :, hi] = (widen(wp[bm, :, hi]) + widen(xb[1])).astype(BF16)
    send(("w", 5), wp.at[bm, :, hi], yb.at[1, :, hi], dev_bm)

    lax.fori_loop(2, 5, grads, 0)
    recv(("m", 0), mr1.at[0], dev_h1)
    mp[h2] = (widen(mp[h2]) + widen(mr1[0])).astype(BF16)
    send(("m", 2), mp.at[h2], mr2, dev_h2)
    lax.fori_loop(5, HEADS, grads, 0)

    recv(("w", 2), yb.at[0, :, hi], dev_bm)
    recv(("w", 3), yb.at[1, :, lo], dev_bp)
    recv(("w", 4), yb.at[0, :, lo], dev_bm)
    recv(("w", 5), yb.at[1, :, hi], dev_bp)

    def w_sum(n, carry):
        cols = pl.ds(pl.multiple_of(n * 256, 256), 256)
        total = wacc[:, cols] + widen(yb[0, :, cols]) + widen(yb[1, :, cols])
        wacc[:, cols] = total
        wa[:, cols] = total.astype(BF16)
        return carry

    lax.fori_loop(0, 12, w_sum, 0)

    def rows_of(a1):
        return pl.ds(pl.multiple_of(a1 * 32, 32), 32)

    send(("v", 0), wa.at[rows_of(ao), lo], xa.at[0], dev_ap)
    send(("v", 1), wa.at[rows_of(ao), hi], xa.at[1], dev_am)
    send(("v", 2), wa.at[rows_of(ap), hi], ya.at[0, :, hi], dev_ap)
    send(("v", 3), wa.at[rows_of(am), lo], ya.at[1, :, lo], dev_am)

    a2a_recv(3, eb, back)

    def finish(h, carry):
        col = ccol[h]
        tail = jnp.exp(col[BLOCK - 1 : BLOCK, :] - col)
        state = state_of(back, h)
        kg = kpart[:, lanes(h)] + tail * mm(v_ref[:, lanes(h)], state, NT)
        vg = vpart[:, lanes(h)] + tail * mm(k_ref[:, lanes(h)], state, NN)
        kg_ref[:, lanes(h)] = kg.astype(BF16)
        vg_ref[:, lanes(h)] = vg.astype(BF16)
        return carry

    lax.fori_loop(0, HEADS, finish, 0)

    recv(("v", 0), xa.at[0], dev_am)
    wa[rows_of(ap), lo] = (widen(wa[rows_of(ap), lo]) + widen(xa[0])).astype(BF16)
    send(("v", 4), wa.at[rows_of(ap), lo], ya.at[0, :, lo], dev_ap)
    recv(("v", 1), xa.at[1], dev_ap)
    wa[rows_of(am), hi] = (widen(wa[rows_of(am), hi]) + widen(xa[1])).astype(BF16)
    send(("v", 5), wa.at[rows_of(am), hi], ya.at[1, :, hi], dev_am)
    recv(("v", 2), ya.at[0, :, hi], dev_am)
    recv(("v", 3), ya.at[1, :, lo], dev_ap)
    recv(("v", 4), ya.at[0, :, lo], dev_am)
    recv(("v", 5), ya.at[1, :, hi], dev_ap)

    def own_rows(z1):
        return pl.ds(pl.multiple_of(a * 32 + z1 * 16, 16), 16)

    def from_both(z1):
        rows = pl.ds(pl.multiple_of(z1 * 16, 16), 16)
        return wacc[own_rows(z1), :] + widen(ya[0, rows, :]) + widen(ya[1, rows, :])

    wa[own_rows(zo), :] = from_both(zo).astype(BF16)
    send(("v", 6), wa.at[own_rows(zo)], xz, dev_z)
    wg_ref[...] = from_both(z)

    recv(("m", 1), mr1.at[1], dev_h1)
    recv(("m", 2), mr2, dev_h2)
    mixed_ref[...] = (macc[...] + widen(mr1[1]) + widen(mr2[...])).astype(BF16)

    recv(("v", 6), xz, dev_z)
    wg_ref[...] += widen(xz[...])

    for copy in started:
        copy.wait_send()
    for n, src, dst in ((0, cf, rf), (1, ef, low), (2, cb, rb), (3, eb, back)):
        a2a_sent(n, src, dst)


def shards(queries, keys, values, log_decay, w_out, grad_out):
    vmem = pl.BlockSpec(memory_space=pltpu.VMEM)
    length = queries.shape[1]
    features = HEADS * DH

    def buf(shape, dtype):
        return pltpu.VMEM(shape, dtype)

    mixed, qg, kg, vg, wg = pl.pallas_call(
        kernel,
        out_shape=(
            jax.ShapeDtypeStruct((length, DOUT // 4), BF16),
            jax.ShapeDtypeStruct((length, features), BF16),
            jax.ShapeDtypeStruct((length, features), BF16),
            jax.ShapeDtypeStruct((length, features), BF16),
            jax.ShapeDtypeStruct((16, DOUT), F32),
        ),
        in_specs=[vmem] * 6,
        out_specs=(vmem,) * 5,
        scratch_shapes=[
            buf((64, 16, DOUT), BF16),
            buf((features, features), BF16),
            buf((HEADS, BLOCK), F32),
            buf((HEADS, BLOCK, DH), F32),
            buf((HEADS, BLOCK, BLOCK), BF16),
            buf((BLOCK, features), F32),
            buf((BLOCK, features), F32),
            buf((BLOCK, features), F32),
            buf((BLOCK, features), BF16),
            buf((BLOCK, features), BF16),
            buf((BLOCK, features), BF16),
            buf((CTX, 40, DH), F32),
            buf((CTX, 40, DH), F32),
            buf((CTX, 32, DH), BF16),
            buf((CTX, 32, DH), BF16),
            buf((CTX, 40, DH), F32),
            buf((CTX, 40, DH), F32),
            buf((CTX, 32, DH), BF16),
            buf((CTX, 32, DH), BF16),
            buf((BLOCK, DOUT), BF16),
            buf((features, BLOCK), BF16),
            buf((512, BLOCK), BF16),
            buf((4, 128, DOUT), BF16),
            buf((128, DOUT), F32),
            buf((2, 128, HALF), BF16),
            buf((2, 128, DOUT), BF16),
            buf((128, DOUT), BF16),
            buf((2, 32, HALF), BF16),
            buf((2, 32, DOUT), BF16),
            buf((16, DOUT), BF16),
            buf((4, BLOCK, 768), BF16),
            buf((BLOCK, 768), F32),
            buf((2, BLOCK, 768), BF16),
            buf((BLOCK, 768), BF16),
            pltpu.SemaphoreType.DMA((72,)),
            pltpu.SemaphoreType.DMA((72,)),
            pltpu.SemaphoreType.DMA((4, CTX)),
            pltpu.SemaphoreType.DMA((4, CTX)),
        ],
        compiler_params=pltpu.CompilerParams(
            collective_id=0, has_side_effects=True, vmem_limit_bytes=60 * 1024 * 1024
        ),
        name="step",
    )(queries[0], keys[0], values[0], log_decay[0], w_out.reshape(16, DOUT), grad_out[0])
    return mixed[None], qg[None], kg[None], vg[None], wg.reshape(2, HEADS, DOUT)


def solution(mesh):
    return jax.shard_map(
        shards,
        mesh=mesh,
        in_specs=(
            P("dp", "ctx", "head"),
            P("dp", "ctx", "head"),
            P("dp", "ctx", "head"),
            P("dp", "head", "ctx"),
            P(("ctx", "dp"), "head", None),
            P("dp", "ctx", None),
        ),
        out_specs=(
            P("dp", "ctx", "head"),
            P("dp", "ctx", "head"),
            P("dp", "ctx", "head"),
            P("dp", "ctx", "head"),
            P(("ctx", "dp"), "head", None),
        ),
        check_vma=False,
    )
```

```python
import jax
import jax.numpy as jnp
from jax import lax
from jax.experimental import pallas as pl
from jax.experimental.pallas import tpu as pltpu
from jax.sharding import PartitionSpec as P

DH = 128
BLOCK = 256
HEADS = 8
DOUT = 3072
HALF = DOUT // 2
CHIPS = 16
SCALE = 1.0 / DH
F32 = jnp.float32
BF16 = jnp.bfloat16
NT = (((1,), (1,)), ((), ()))
NN = (((1,), (0,)), ((), ()))
TN = (((0,), (0,)), ((), ()))


def mm(a, b, dims):
    return lax.dot_general(a, b, dims, preferred_element_type=F32)


class Ids:
    def __init__(self):
        self.names = {}

    def __call__(self, *name):
        return self.names.setdefault(name, len(self.names))


def kernel(
    q_in, k_in, v_in, ld_in, w_in, go_in,
    mixed_out, qg_out, kg_out, vg_out, wg_out,
    q_ref, k_ref, v_ref, ld_ref, go_ref, mixed_ref, qg_ref, kg_ref, vg_ref, wg_ref,
    panel, pt, cum, ccol, probs, intra, kpart, vpart, att, attp, gh,
    cf, sf, tf, rf, ef, inf, lowf, low, cb, sb, tb, rb, eb, inb, lowb, back,
    go_sib, att_t, att_sib,
    wp, xb, yb, wacc, wa, xa, ya, xz,
    mp, macc, mr1, mr2,
    ssem, rsem, a2a_s, a2a_r, isem, osem,
):
    ctx, head, dp = lax.axis_index("ctx"), lax.axis_index("head"), lax.axis_index("dp")
    core, chip = ctx % 2, ctx // 2
    x, y = chip % 4, ctx // 8
    a = x * (1 - core) + y * core
    b = y * (1 - core) + x * core
    ap, am, ao = (a + 1) % 4, (a + 3) % 4, (a + 2) % 4
    bp, bm, bo = (b + 1) % 4, (b + 3) % 4, (b + 2) % 4
    z, zo = dp, 1 - dp

    def at(a1, b1):
        x1 = a1 * (1 - core) + b1 * core
        y1 = b1 * (1 - core) + a1 * core
        return ((y1 * 4 + x1) * 2 + core, head, dp)

    dev_ap, dev_am, dev_bp, dev_bm = at(ap, b), at(am, b), at(a, bp), at(a, bm)
    dev_sib = (ctx + 1 - 2 * core, head, dp)
    dev_z = (ctx, head, zo)
    h1 = head + 1 - 2 * (head % 2)
    h2 = (head + 2) % 4
    h3 = (h1 + 2) % 4
    dev_h1, dev_h2 = (ctx, h1, dp), (ctx, h2, dp)

    ids = Ids()
    started = []

    def xfer(name, src, dst, dev):
        i = ids(*name)
        return pltpu.make_async_remote_copy(
            src_ref=src, dst_ref=dst, send_sem=ssem.at[i], recv_sem=rsem.at[i],
            device_id=dev, device_id_type=pl.DeviceIdType.MESH,
        )

    def send(name, src, dst, dev):
        copy = xfer(name, src, dst, dev)
        copy.start()
        started.append(copy)

    def recv(name, ref, dev):
        xfer(name, ref, ref, dev).wait_recv()

    def slot(a1, b1, z1):
        return core * 32 + z1 * 16 + b1 * 4 + a1

    mine = slot(a, b, z)
    pairs = ((w_in, panel.at[mine]), (ld_in, ld_ref), (k_in, k_ref), (v_in, v_ref), (q_in, q_ref), (go_in, go_ref))
    loads = [pltpu.make_async_copy(src, dst, isem.at[i]) for i, (src, dst) in enumerate(pairs)]
    for load in loads:
        load.start()

    barrier = pltpu.get_barrier_semaphore()

    def greet(i, carry):
        pl.semaphore_signal(
            barrier, inc=1, device_id=((chip + i) % CHIPS * 2 + core, head, dp), device_id_type=pl.DeviceIdType.MESH
        )
        return carry

    lax.fori_loop(1, CHIPS, greet, 0)
    for dev in (dev_sib, dev_z, dev_h1, dev_h2):
        pl.semaphore_signal(barrier, inc=1, device_id=dev, device_id_type=pl.DeviceIdType.MESH)
    pl.semaphore_wait(barrier, CHIPS - 1 + 4)

    def whole(s):
        return panel.at[s]

    def part(s, h):
        return panel.at[s, :, pl.ds(h * HALF, HALF)]

    a_of = {0: a, 1: am, 2: ap, 3: ao}

    def b_sends(zi, k):
        zz = (z, zo)[zi]
        ref = whole(slot(a_of[k], b, zz))
        send(("bp", zi, k), ref, ref, dev_bp)
        send(("bm", zi, k), ref, ref, dev_bm)

    def a_sends(zi):
        ref = whole(slot(a, b, (z, zo)[zi]))
        send(("ap", zi), ref, ref, dev_ap)
        send(("am", zi), ref, ref, dev_am)

    def step_a(zi):
        zz = (z, zo)[zi]
        left, right = slot(am, b, zz), slot(ap, b, zz)
        recv(("ap", zi), whole(left), dev_am)
        send(("afp", zi), part(left, 0), part(left, 0), dev_ap)
        b_sends(zi, 1)
        recv(("am", zi), whole(right), dev_ap)
        send(("afm", zi), part(right, 1), part(right, 1), dev_am)
        b_sends(zi, 2)

    def step_ao(zi):
        far = slot(ao, b, (z, zo)[zi])
        recv(("afp", zi), part(far, 0), dev_am)
        recv(("afm", zi), part(far, 1), dev_ap)
        b_sends(zi, 3)
        sib_send(zi, 0)

    def step_b(zi, k):
        zz = (z, zo)[zi]
        below, above = slot(a_of[k], bm, zz), slot(a_of[k], bp, zz)
        recv(("bp", zi, k), whole(below), dev_bm)
        send(("bfp", zi, k), part(below, 0), part(below, 0), dev_bp)
        recv(("bm", zi, k), whole(above), dev_bp)
        send(("bfm", zi, k), part(above, 1), part(above, 1), dev_bm)

    def step_bo(zi, k):
        far = slot(a_of[k], bo, (z, zo)[zi])
        recv(("bfp", zi, k), part(far, 0), dev_bm)
        recv(("bfm", zi, k), part(far, 1), dev_bp)

    def step_z():
        recv(("z",), whole(slot(a, b, zo)), dev_z)
        a_sends(1)
        b_sends(1, 0)

    def row(c1, b1, z1):
        return panel.at[pl.ds(c1 * 32 + z1 * 16 + b1 * 4, 4)]

    def sib_send(zi, k):
        ref = row(core, (b, bm, bp, bo)[k], (z, zo)[zi])
        send(("sib", zi, k), ref, ref, dev_sib)

    def sib_recv(zi, k):
        recv(("sib", zi, k), row(1 - core, (a, am, ap, ao)[k], (z, zo)[zi]), dev_sib)

    loads[0].wait()
    send(("z",), whole(mine), whole(mine), dev_z)
    a_sends(0)
    b_sends(0, 0)
    for load in loads[1:4]:
        load.wait()

    t_row = lax.broadcasted_iota(jnp.int32, (BLOCK, BLOCK), 0)
    t_col = lax.broadcasted_iota(jnp.int32, (BLOCK, BLOCK), 1)
    upper = (t_row <= t_col).astype(F32)
    cum[...] = jnp.dot(ld_ref[...], upper, precision=lax.Precision.HIGHEST, preferred_element_type=F32)

    def lanes(h):
        return pl.ds(pl.multiple_of(h * DH, DH), DH)

    def weights(h):
        col = ccol[h]
        spread = jnp.concatenate([col, col], axis=1) - cum[pl.ds(h, 1), :]
        rows = lax.broadcasted_iota(jnp.int32, (BLOCK, BLOCK), 0)
        cols = lax.broadcasted_iota(jnp.int32, (BLOCK, BLOCK), 1)
        return jnp.exp(jnp.where(rows >= cols, spread, -jnp.inf))

    def pieces(buf, h, total, decay):
        for r in range(4):
            buf[h * 4 + r, 0:32, :] = total[r * 32 : (r + 1) * 32]
            buf[h * 4 + r, 32:40, :] = jnp.broadcast_to(decay, (8, DH))

    def fwd_share(h, carry):
        wide = jnp.broadcast_to(cum[pl.ds(h, 1), :], (DH, BLOCK))
        col = wide.T
        ccol[h] = col
        last = col[BLOCK - 1 : BLOCK, :]
        kw = (k_ref[:, lanes(h)].astype(F32) * jnp.exp(last - col)).astype(BF16)
        pieces(cf, h, mm(kw, v_ref[:, lanes(h)], TN), jnp.exp(last))
        return carry

    def halves(own, sib, j, first):
        p, o = own[core * CHIPS + j], sib[j]
        return jnp.where(core == first, p, o), jnp.where(core == first, o, p)

    def own_half(buf):
        return buf.at[pl.ds(core * CHIPS, CHIPS)]

    def other_half(buf):
        return buf.at[pl.ds((1 - core) * CHIPS, CHIPS)]

    def merge(own, sib, out, first):
        def go(j, carry):
            p, s = halves(own, sib, j, first)
            out[j, 0:32, :] = s[32:33] * p[0:32] + s[0:32]
            out[j, 32:40, :] = s[32:40] * p[32:40]
            return carry

        lax.fori_loop(0, CHIPS, go, 0)

    def split(own, sib, got, out, out_sib, first):
        def go(j, carry):
            p, _ = halves(own, sib, j, first)
            early = got[j].astype(F32)
            late = p[32:33] * early + p[0:32]
            out[core * CHIPS + j] = jnp.where(core == first, early, late).astype(BF16)
            out_sib[j] = jnp.where(core == first, late, early).astype(BF16)
            return carry

        lax.fori_loop(0, CHIPS, go, 0)

    def a2a(n, src, dst, i, out):
        other = (chip + i) % CHIPS if out else (chip + CHIPS - i) % CHIPS
        return pltpu.make_async_remote_copy(
            src_ref=src.at[other], dst_ref=dst.at[chip if out else other],
            send_sem=a2a_s.at[n, i], recv_sem=a2a_r.at[n, i],
            device_id=(other * 2 + core, head, dp), device_id_type=pl.DeviceIdType.MESH,
        )

    def a2a_start(n, src, dst):
        def go(i, carry):
            a2a(n, src, dst, i, True).start()
            return carry

        lax.fori_loop(1, CHIPS, go, 0)
        dst[chip] = src[chip]

    def a2a_recv(n, src, dst):
        def go(i, carry):
            a2a(n, src, dst, i, False).wait_recv()
            return carry

        lax.fori_loop(1, CHIPS, go, 0)

    def a2a_sent(n, src, dst):
        def go(i, carry):
            a2a(n, src, dst, i, True).wait_send()
            return carry

        lax.fori_loop(1, CHIPS, go, 0)

    def scan(got, out, reverse):
        def go(i, state):
            at_chip = CHIPS - 1 - i if reverse else i
            out[at_chip] = state.astype(BF16)
            return state * got[at_chip, 32:33, :] + got[at_chip, 0:32, :]

        lax.fori_loop(0, CHIPS, go, jnp.zeros((32, DH), F32))

    def state_of(buf, h):
        return buf[pl.ds(h * 4, 4)].reshape(DH, DH)

    lax.fori_loop(0, HEADS, fwd_share, 0)
    send(("f", 0), other_half(cf), sf, dev_sib)
    step_a(0)
    recv(("f", 0), sf, dev_sib)
    merge(cf, sf, tf, 0)
    a2a_start(0, tf, rf)
    loads[4].wait()
    loads[5].wait()
    send(("go",), go_ref, go_sib, dev_sib)

    def inside(h, carry):
        scores = mm(q_ref[:, lanes(h)], k_ref[:, lanes(h)], NT)
        p = (scores * SCALE * weights(h)).astype(BF16)
        probs[h] = p
        intra[:, lanes(h)] = mm(p, v_ref[:, lanes(h)], NN)
        return carry

    lax.fori_loop(0, 2, inside, 0)
    step_ao(0)
    step_z()
    step_b(0, 0)
    lax.fori_loop(2, 5, inside, 0)
    step_b(0, 1)
    step_b(0, 2)
    a2a_recv(0, tf, rf)
    scan(rf, ef, False)
    a2a_start(1, ef, inf)
    step_a(1)
    lax.fori_loop(5, HEADS, inside, 0)
    step_b(0, 3)
    sib_send(0, 1)
    sib_send(0, 2)
    step_ao(1)
    step_b(1, 0)

    a2a_recv(1, ef, inf)
    split(cf, sf, inf, low, lowf, 0)
    send(("f", 1), lowf, own_half(low), dev_sib)

    r = lax.broadcasted_iota(jnp.int32, (1024, DH), 0)
    place = r >> 4
    pc, pz, pb, pa = place >> 5, (place >> 4) & 1, (place >> 2) & 3, place & 3
    px = jnp.where(pc == 0, pa, pb)
    py = jnp.where(pc == 0, pb, pa)
    feature = 2 * ((((py * 4) + px) * 2 + pc) * 2 + pz) + ((r >> 3) & 1)
    lane = lax.broadcasted_iota(jnp.int32, (1024, DH), 1)
    same = feature == lane
    for h in range(HEADS):
        pt[:, h * DH : (h + 1) * DH] = jnp.where(same & ((r & 7) == h), 1.0, 0.0).astype(BF16)

    step_b(1, 1)
    step_b(1, 2)
    recv(("f", 1), other_half(low), dev_sib)

    def attend(h, carry):
        inter = mm(q_ref[:, lanes(h)], state_of(low, h), NN)
        factor = SCALE * jnp.exp(ccol[h])
        att[:, lanes(h)] = (intra[:, lanes(h)] + inter * factor).astype(BF16)
        return carry

    lax.fori_loop(0, HEADS, attend, 0)
    step_b(1, 3)
    sib_send(1, 1)
    sib_send(1, 2)

    def turn(i, carry):
        rows = pl.ds(pl.multiple_of(i * 256, 256), 256)
        att_t[rows, :] = mm(pt[rows, :], att[...], NT).astype(BF16)
        attp[:, rows] = mm(att[...], pt[rows, :], NT).astype(BF16)
        return carry

    lax.fori_loop(0, 4, turn, 0)
    other_rows = pl.ds(pl.multiple_of((1 - core) * 512, 512), 512)
    send(("att",), att_t.at[other_rows], att_sib, dev_sib)
    for k in range(4):
        step_bo(0, k)
    sib_send(0, 3)

    recv(("go",), go_sib, dev_sib)
    recv(("att",), att_sib, dev_sib)
    lo, hi = pl.ds(0, HALF), pl.ds(HALF, HALF)

    def widen(ref):
        return ref.astype(F32)

    def rows_b(b1):
        return pl.ds(pl.multiple_of(b1 * 64, 64), 64)

    def rows_a(a1):
        return pl.ds(pl.multiple_of(a1 * 16, 16), 16)

    def w_block(zi):
        zz = (zo, z)[zi]
        own = pl.ds(pl.multiple_of(core * 512 + zz * 256, 256), 256)
        sib = pl.ds(pl.multiple_of(zz * 256, 256), 256)

        def go(n, carry):
            cols = pl.ds(pl.multiple_of(n * 256, 256), 256)
            value = mm(att_t[own, :], go_ref[:, cols], NN) + mm(att_sib[sib, :], go_sib[:, cols], NN)
            wp[zi, :, cols] = value.astype(BF16)
            return carry

        lax.fori_loop(0, 12, go, 0)

    def w_first(zi):
        w_block(zi)
        send(("w", zi, 0), wp.at[zi, rows_b(bo), lo], xb.at[zi, 0], dev_bp)
        send(("w", zi, 1), wp.at[zi, rows_b(bo), hi], xb.at[zi, 1], dev_bm)
        send(("w", zi, 2), wp.at[zi, rows_b(bp), hi], yb.at[zi, 0, :, hi], dev_bp)
        send(("w", zi, 3), wp.at[zi, rows_b(bm), lo], yb.at[zi, 1, :, lo], dev_bm)

    def w_relay(zi):
        recv(("w", zi, 0), xb.at[zi, 0], dev_bm)
        wp[zi, rows_b(bp), lo] = (widen(wp[zi, rows_b(bp), lo]) + widen(xb[zi, 0])).astype(BF16)
        send(("w", zi, 4), wp.at[zi, rows_b(bp), lo], yb.at[zi, 0, :, lo], dev_bp)
        recv(("w", zi, 1), xb.at[zi, 1], dev_bp)
        wp[zi, rows_b(bm), hi] = (widen(wp[zi, rows_b(bm), hi]) + widen(xb[zi, 1])).astype(BF16)
        send(("w", zi, 5), wp.at[zi, rows_b(bm), hi], yb.at[zi, 1, :, hi], dev_bm)

    def v_first(zi):
        recv(("w", zi, 2), yb.at[zi, 0, :, hi], dev_bm)
        recv(("w", zi, 3), yb.at[zi, 1, :, lo], dev_bp)
        recv(("w", zi, 4), yb.at[zi, 0, :, lo], dev_bm)
        recv(("w", zi, 5), yb.at[zi, 1, :, hi], dev_bp)

        def go(n, carry):
            cols = pl.ds(pl.multiple_of(n * 256, 256), 256)
            total = widen(wp[zi, rows_b(b), cols]) + widen(yb[zi, 0, :, cols]) + widen(yb[zi, 1, :, cols])
            wacc[zi, :, cols] = total
            wa[zi, :, cols] = total.astype(BF16)
            return carry

        lax.fori_loop(0, 12, go, 0)
        send(("v", zi, 0), wa.at[zi, rows_a(ao), lo], xa.at[zi, 0], dev_ap)
        send(("v", zi, 1), wa.at[zi, rows_a(ao), hi], xa.at[zi, 1], dev_am)
        send(("v", zi, 2), wa.at[zi, rows_a(ap), hi], ya.at[zi, 0, :, hi], dev_ap)
        send(("v", zi, 3), wa.at[zi, rows_a(am), lo], ya.at[zi, 1, :, lo], dev_am)

    def v_relay(zi):
        recv(("v", zi, 0), xa.at[zi, 0], dev_am)
        wa[zi, rows_a(ap), lo] = (widen(wa[zi, rows_a(ap), lo]) + widen(xa[zi, 0])).astype(BF16)
        send(("v", zi, 4), wa.at[zi, rows_a(ap), lo], ya.at[zi, 0, :, lo], dev_ap)
        recv(("v", zi, 1), xa.at[zi, 1], dev_ap)
        wa[zi, rows_a(am), hi] = (widen(wa[zi, rows_a(am), hi]) + widen(xa[zi, 1])).astype(BF16)
        send(("v", zi, 5), wa.at[zi, rows_a(am), hi], ya.at[zi, 1, :, hi], dev_am)

    def v_last(zi):
        recv(("v", zi, 2), ya.at[zi, 0, :, hi], dev_am)
        recv(("v", zi, 3), ya.at[zi, 1, :, lo], dev_ap)
        recv(("v", zi, 4), ya.at[zi, 0, :, lo], dev_am)
        recv(("v", zi, 5), ya.at[zi, 1, :, hi], dev_ap)
        return wacc[zi, rows_a(a), :] + widen(ya[zi, 0]) + widen(ya[zi, 1])

    w_first(0)
    w_first(1)

    for k in range(4):
        step_bo(1, k)
    sib_send(1, 3)
    for zi in range(2):
        for k in range(4):
            sib_recv(zi, k)

    def mix(dest, store):
        def go(n, carry):
            cols = pl.ds(pl.multiple_of(dest * 768 + n * 256, 256), 256)
            w = panel[:, :, cols].reshape(1024, 256)
            store(pl.ds(pl.multiple_of(n * 256, 256), 256), mm(attp[...], w, NN))
            return carry

        lax.fori_loop(0, 3, go, 0)

    def store_at(dest):
        def store(cols, value):
            mp[dest, :, cols] = value.astype(BF16)

        return store

    def store_own(cols, value):
        macc[:, cols] = value

    mix(h3, store_at(h3))
    send(("m", 0), mp.at[h3], mr1.at[0], dev_h1)
    mix(h1, store_at(h1))
    send(("m", 1), mp.at[h1], mr1.at[1], dev_h1)

    def heads_grad(i, carry):
        rows = panel[pl.ds(i * 16, 16)].reshape(256, DOUT)
        cols = pl.ds(pl.multiple_of(i * 256, 256), 256)
        gh[:, cols] = mm(go_ref[...], rows, NT).astype(BF16)
        return carry

    lax.fori_loop(0, 4, heads_grad, 0)
    by_head = []
    for n in range(4):
        by_head.append(mm(gh[...], pt[:, n * 256 : (n + 1) * 256], NN).astype(BF16))
    for n in range(4):
        gh[:, n * 256 : (n + 1) * 256] = by_head[n]

    def bwd_share(h, carry):
        qw = (q_ref[:, lanes(h)].astype(F32) * (SCALE * jnp.exp(ccol[h]))).astype(BF16)
        last = ccol[h, BLOCK - 1 : BLOCK, :]
        pieces(cb, h, mm(qw, gh[:, lanes(h)], TN), jnp.exp(last))
        return carry

    lax.fori_loop(0, HEADS, bwd_share, 0)
    send(("k", 0), other_half(cb), sb, dev_sib)
    w_relay(0)
    recv(("k", 0), sb, dev_sib)
    merge(cb, sb, tb, 1)
    a2a_start(2, tb, rb)
    w_relay(1)
    mix(h2, store_at(h2))

    def grads(h, carry):
        g, kk, vv, qq = gh[:, lanes(h)], k_ref[:, lanes(h)], v_ref[:, lanes(h)], q_ref[:, lanes(h)]
        dp_h = (mm(g, vv, NT) * SCALE * weights(h)).astype(BF16)
        factor = SCALE * jnp.exp(ccol[h])
        qg = mm(dp_h, kk, NN) + mm(g, state_of(low, h), NT) * factor
        qg_ref[:, lanes(h)] = qg.astype(BF16)
        kpart[:, lanes(h)] = mm(dp_h, qq, TN)
        vpart[:, lanes(h)] = mm(probs[h], g, TN)
        return carry

    lax.fori_loop(0, 2, grads, 0)
    v_first(0)
    recv(("m", 0), mr1.at[0], dev_h1)
    mp[h2] = (widen(mp[h2]) + widen(mr1[0])).astype(BF16)
    send(("m", 2), mp.at[h2], mr2, dev_h2)
    a2a_recv(2, tb, rb)
    scan(rb, eb, True)
    a2a_start(3, eb, inb)
    lax.fori_loop(2, 5, grads, 0)
    v_relay(0)
    v_first(1)
    lax.fori_loop(5, HEADS, grads, 0)
    wa[0, rows_a(a), :] = v_last(0).astype(BF16)
    send(("vz",), wa.at[0, rows_a(a)], xz, dev_z)
    v_relay(1)

    a2a_recv(3, eb, inb)
    split(cb, sb, inb, back, lowb, 1)
    send(("k", 1), lowb, own_half(back), dev_sib)
    outs = [
        pltpu.make_async_copy(src, dst, osem.at[i])
        for i, (src, dst) in enumerate(
            ((qg_ref, qg_out), (kg_ref, kg_out), (vg_ref, vg_out), (mixed_ref, mixed_out), (wg_ref, wg_out))
        )
    ]
    outs[0].start()
    mix(head, store_own)
    recv(("k", 1), other_half(back), dev_sib)

    def finish(h, carry):
        col = ccol[h]
        tail = jnp.exp(col[BLOCK - 1 : BLOCK, :] - col)
        state = state_of(back, h)
        kg = kpart[:, lanes(h)] + tail * mm(v_ref[:, lanes(h)], state, NT)
        vg = vpart[:, lanes(h)] + tail * mm(k_ref[:, lanes(h)], state, NN)
        kg_ref[:, lanes(h)] = kg.astype(BF16)
        vg_ref[:, lanes(h)] = vg.astype(BF16)
        return carry

    lax.fori_loop(0, HEADS, finish, 0)
    outs[1].start()
    outs[2].start()

    wg_ref[...] = v_last(1)
    recv(("vz",), xz, dev_z)
    wg_ref[...] += widen(xz[...])
    outs[4].start()

    recv(("m", 1), mr1.at[1], dev_h1)
    recv(("m", 2), mr2, dev_h2)
    mixed_ref[...] = (macc[...] + widen(mr1[1]) + widen(mr2[...])).astype(BF16)
    outs[3].start()

    for copy in started:
        copy.wait_send()
    for n, src, dst in ((0, tf, rf), (1, ef, inf), (2, tb, rb), (3, eb, inb)):
        a2a_sent(n, src, dst)
    for out in outs:
        out.wait()


def hand_out(*refs):
    n = len(refs) // 3
    given, out, held, sems = refs[:n], refs[n : 2 * n], refs[2 * n : 3 * n], refs[-1]
    first = [pltpu.make_async_copy(given[i], held[i], sems.at[0, i]) for i in range(n)]
    second = [pltpu.make_async_copy(held[i], out[i], sems.at[1, i]) for i in range(n)]
    for copy in first:
        copy.start()
    for i in range(n):
        first[i].wait()
        second[i].start()
    for copy in second:
        copy.wait()


def shards(queries, keys, values, log_decay, w_out, grad_out):
    hbm = pl.BlockSpec(memory_space=pl.ANY)
    length = queries.shape[1]
    features = HEADS * DH
    shapes = (
        jax.ShapeDtypeStruct((length, DOUT // 4), BF16),
        jax.ShapeDtypeStruct((length, features), BF16),
        jax.ShapeDtypeStruct((length, features), BF16),
        jax.ShapeDtypeStruct((length, features), BF16),
        jax.ShapeDtypeStruct((16, DOUT), F32),
    )
    whole = pltpu.VMEM((length, features), BF16)
    wide = pltpu.VMEM((length, features), F32)
    piece = pltpu.VMEM((CHIPS, 40, DH), F32)
    state = pltpu.VMEM((CHIPS, 32, DH), BF16)
    scan = [
        pltpu.VMEM((2 * CHIPS, 40, DH), F32), piece, piece, piece,
        state, state, state, pltpu.VMEM((2 * CHIPS, 32, DH), BF16),
    ]

    results = pl.pallas_call(
        kernel,
        out_shape=shapes,
        in_specs=[hbm] * 6,
        out_specs=(hbm,) * 5,
        scratch_shapes=[
            whole,
            whole,
            whole,
            pltpu.VMEM((HEADS, BLOCK), F32),
            pltpu.VMEM((BLOCK, DOUT), BF16),
            pltpu.VMEM((BLOCK, DOUT // 4), BF16),
            whole,
            whole,
            whole,
            pltpu.VMEM((16, DOUT), F32),
            pltpu.VMEM((64, 16, DOUT), BF16),
            pltpu.VMEM((features, features), BF16),
            pltpu.VMEM((HEADS, BLOCK), F32),
            pltpu.VMEM((HEADS, BLOCK, DH), F32),
            pltpu.VMEM((HEADS, BLOCK, BLOCK), BF16),
            wide,
            wide,
            wide,
            whole,
            whole,
            whole,
            *scan,
            *scan,
            pltpu.VMEM((BLOCK, DOUT), BF16),
            pltpu.VMEM((features, BLOCK), BF16),
            pltpu.VMEM((512, BLOCK), BF16),
            pltpu.VMEM((2, 256, DOUT), BF16),
            pltpu.VMEM((2, 2, 64, HALF), BF16),
            pltpu.VMEM((2, 2, 64, DOUT), BF16),
            pltpu.VMEM((2, 64, DOUT), F32),
            pltpu.VMEM((2, 64, DOUT), BF16),
            pltpu.VMEM((2, 2, 16, HALF), BF16),
            pltpu.VMEM((2, 2, 16, DOUT), BF16),
            pltpu.VMEM((16, DOUT), BF16),
            pltpu.VMEM((4, BLOCK, 768), BF16),
            pltpu.VMEM((BLOCK, 768), F32),
            pltpu.VMEM((2, BLOCK, 768), BF16),
            pltpu.VMEM((BLOCK, 768), BF16),
            pltpu.SemaphoreType.DMA((88,)),
            pltpu.SemaphoreType.DMA((88,)),
            pltpu.SemaphoreType.DMA((4, CHIPS)),
            pltpu.SemaphoreType.DMA((4, CHIPS)),
            pltpu.SemaphoreType.DMA((6,)),
            pltpu.SemaphoreType.DMA((5,)),
        ],
        compiler_params=pltpu.CompilerParams(
            collective_id=0, has_side_effects=True, vmem_limit_bytes=60 * 1024 * 1024
        ),
        name="step",
    )(queries[0], keys[0], values[0], log_decay[0], w_out.reshape(16, DOUT), grad_out[0])
    mixed, qg, kg, vg, wg = pl.pallas_call(
        hand_out,
        out_shape=shapes,
        in_specs=[hbm] * 5,
        out_specs=(hbm,) * 5,
        scratch_shapes=[*(pltpu.VMEM(s.shape, s.dtype) for s in shapes), pltpu.SemaphoreType.DMA((2, 5))],
        compiler_params=pltpu.CompilerParams(vmem_limit_bytes=60 * 1024 * 1024),
        name="hand_out",
    )(*results)
    return mixed[None], qg[None], kg[None], vg[None], wg.reshape(2, HEADS, DOUT)


def solution(mesh):
    return jax.shard_map(
        shards,
        mesh=mesh,
        in_specs=(
            P("dp", "ctx", "head"),
            P("dp", "ctx", "head"),
            P("dp", "ctx", "head"),
            P("dp", "head", "ctx"),
            P(("ctx", "dp"), "head", None),
            P("dp", "ctx", None),
        ),
        out_specs=(
            P("dp", "ctx", "head"),
            P("dp", "ctx", "head"),
            P("dp", "ctx", "head"),
            P("dp", "ctx", "head"),
            P(("ctx", "dp"), "head", None),
        ),
        check_vma=False,
    )
```

```python
import jax
import jax.numpy as jnp
from jax import lax
from jax.experimental import pallas as pl
from jax.experimental.pallas import tpu as pltpu
from jax.sharding import PartitionSpec as P

DH = 128
BLOCK = 256
HEADS = 8
DOUT = 3072
HALF = DOUT // 2
CHIPS = 16
SCALE = 1.0 / DH
F32 = jnp.float32
BF16 = jnp.bfloat16
NT = (((1,), (1,)), ((), ()))
NN = (((1,), (0,)), ((), ()))
TN = (((0,), (0,)), ((), ()))


def mm(a, b, dims):
    return lax.dot_general(a, b, dims, preferred_element_type=F32)


class Ids:
    def __init__(self):
        self.names = {}

    def __call__(self, *name):
        return self.names.setdefault(name, len(self.names))


def kernel(
    q_in, k_in, v_in, ld_in, w_in, go_in,
    mixed_out, qg_out, kg_out, vg_out, wg_out,
    q_ref, k_ref, v_ref, ld_ref, go_ref, mixed_ref, qg_ref, kg_ref, vg_ref, wg_ref,
    panel, pt, cum, ccol, probs, intra, kpart, vpart, att, attp, gh,
    cf, sf, tf, rf, ef, inf, lowf, low, cb, sb, tb, rb, eb, inb, lowb, back,
    go_sib, att_t, att_sib,
    wp, xb, yb, wacc, wa, ya, xz,
    mp, macc, mr1, mr2,
    ssem, rsem, a2a_s, a2a_r, isem, osem,
):
    ctx, head, dp = lax.axis_index("ctx"), lax.axis_index("head"), lax.axis_index("dp")
    core, chip = ctx % 2, ctx // 2
    x, y = chip % 4, ctx // 8
    a = x * (1 - core) + y * core
    b = y * (1 - core) + x * core
    ap, am, ao = (a + 1) % 4, (a + 3) % 4, (a + 2) % 4
    bp, bm, bo = (b + 1) % 4, (b + 3) % 4, (b + 2) % 4
    z, zo = dp, 1 - dp

    def at(a1, b1):
        x1 = a1 * (1 - core) + b1 * core
        y1 = b1 * (1 - core) + a1 * core
        return ((y1 * 4 + x1) * 2 + core, head, dp)

    dev_ap, dev_am, dev_ao, dev_bp, dev_bm = at(ap, b), at(am, b), at(ao, b), at(a, bp), at(a, bm)
    dev_sib = (ctx + 1 - 2 * core, head, dp)
    dev_z = (ctx, head, zo)
    h1 = head + 1 - 2 * (head % 2)
    h2 = (head + 2) % 4
    h3 = (h1 + 2) % 4
    dev_h1, dev_h2 = (ctx, h1, dp), (ctx, h2, dp)

    ids = Ids()
    started = []

    def xfer(name, src, dst, dev):
        i = ids(*name)
        return pltpu.make_async_remote_copy(
            src_ref=src, dst_ref=dst, send_sem=ssem.at[i], recv_sem=rsem.at[i],
            device_id=dev, device_id_type=pl.DeviceIdType.MESH,
        )

    def send(name, src, dst, dev):
        copy = xfer(name, src, dst, dev)
        copy.start()
        started.append(copy)

    def recv(name, ref, dev):
        xfer(name, ref, ref, dev).wait_recv()

    def slot(a1, b1, z1):
        return core * 32 + z1 * 16 + b1 * 4 + a1

    mine = slot(a, b, z)
    pairs = ((w_in, panel.at[mine]), (ld_in, ld_ref), (k_in, k_ref), (v_in, v_ref), (q_in, q_ref), (go_in, go_ref))
    loads = [pltpu.make_async_copy(src, dst, isem.at[i]) for i, (src, dst) in enumerate(pairs)]
    for load in loads:
        load.start()

    barrier = pltpu.get_barrier_semaphore()

    def greet(i, carry):
        pl.semaphore_signal(
            barrier, inc=1, device_id=((chip + i) % CHIPS * 2 + core, head, dp), device_id_type=pl.DeviceIdType.MESH
        )
        return carry

    lax.fori_loop(1, CHIPS, greet, 0)
    for dev in (dev_sib, dev_z, dev_h1, dev_h2):
        pl.semaphore_signal(barrier, inc=1, device_id=dev, device_id_type=pl.DeviceIdType.MESH)
    for load in loads[1:4]:
        load.wait()

    t_row = lax.broadcasted_iota(jnp.int32, (BLOCK, BLOCK), 0)
    t_col = lax.broadcasted_iota(jnp.int32, (BLOCK, BLOCK), 1)
    upper = (t_row <= t_col).astype(F32)
    cum[...] = jnp.dot(ld_ref[...], upper, precision=lax.Precision.HIGHEST, preferred_element_type=F32)

    def heads(first, last, body):
        lax.fori_loop(first, last, body, 0, unroll=2 if (last - first) % 2 == 0 else 1)

    def lanes(h):
        return pl.ds(pl.multiple_of(h * DH, DH), DH)

    def pieces(buf, h, total, decay):
        for r in range(4):
            buf[h * 4 + r, 0:32, :] = total[r * 32 : (r + 1) * 32]
            buf[h * 4 + r, 32:40, :] = jnp.broadcast_to(decay, (8, DH))

    def fwd_share(h, carry):
        wide = jnp.broadcast_to(cum[pl.ds(h, 1), :], (DH, BLOCK))
        col = wide.T
        ccol[h] = col
        last = col[BLOCK - 1 : BLOCK, :]
        kw = (k_ref[:, lanes(h)].astype(F32) * jnp.exp(last - col)).astype(BF16)
        pieces(cf, h, mm(kw, v_ref[:, lanes(h)], TN), jnp.exp(last))
        return carry

    heads(0, 4, fwd_share)
    pl.semaphore_wait(barrier, CHIPS - 1 + 4)

    def whole(s):
        return panel.at[s]

    def part(s, h):
        return panel.at[s, :, pl.ds(h * HALF, HALF)]

    a_of = {0: a, 1: am, 2: ap, 3: ao}

    def b_sends(zi, k):
        zz = (z, zo)[zi]
        ref = whole(slot(a_of[k], b, zz))
        send(("bp", zi, k), ref, ref, dev_bp)
        send(("bm", zi, k), ref, ref, dev_bm)

    def a_sends(zi):
        ref = whole(slot(a, b, (z, zo)[zi]))
        send(("ap", zi), ref, ref, dev_ap)
        send(("am", zi), ref, ref, dev_am)
        send(("ao", zi), ref, ref, dev_ao)

    def step_a(zi):
        zz = (z, zo)[zi]
        left, right = slot(am, b, zz), slot(ap, b, zz)
        recv(("ap", zi), whole(left), dev_am)
        b_sends(zi, 1)
        recv(("am", zi), whole(right), dev_ap)
        b_sends(zi, 2)

    def step_ao(zi):
        far = slot(ao, b, (z, zo)[zi])
        recv(("ao", zi), whole(far), dev_ao)
        b_sends(zi, 3)
        sib_send(zi, 0)

    def step_b(zi, k):
        zz = (z, zo)[zi]
        below, above = slot(a_of[k], bm, zz), slot(a_of[k], bp, zz)
        recv(("bp", zi, k), whole(below), dev_bm)
        send(("bfp", zi, k), part(below, 0), part(below, 0), dev_bp)
        recv(("bm", zi, k), whole(above), dev_bp)
        send(("bfm", zi, k), part(above, 1), part(above, 1), dev_bm)

    def step_bo(zi, k):
        far = slot(a_of[k], bo, (z, zo)[zi])
        recv(("bfp", zi, k), part(far, 0), dev_bm)
        recv(("bfm", zi, k), part(far, 1), dev_bp)

    def step_z():
        recv(("z",), whole(slot(a, b, zo)), dev_z)
        a_sends(1)
        b_sends(1, 0)

    def row(c1, b1, z1):
        return panel.at[pl.ds(c1 * 32 + z1 * 16 + b1 * 4, 4)]

    def sib_send(zi, k):
        ref = row(core, (b, bm, bp, bo)[k], (z, zo)[zi])
        send(("sib", zi, k), ref, ref, dev_sib)

    def sib_recv(zi, k):
        recv(("sib", zi, k), row(1 - core, (a, am, ap, ao)[k], (z, zo)[zi]), dev_sib)

    loads[0].wait()
    send(("z",), whole(mine), whole(mine), dev_z)
    a_sends(0)
    b_sends(0, 0)
    def weights(h):
        col = ccol[h]
        spread = jnp.concatenate([col, col], axis=1) - cum[pl.ds(h, 1), :]
        rows = lax.broadcasted_iota(jnp.int32, (BLOCK, BLOCK), 0)
        cols = lax.broadcasted_iota(jnp.int32, (BLOCK, BLOCK), 1)
        return jnp.exp(jnp.where(rows >= cols, spread, -jnp.inf))

    def halves(own, sib, j, first):
        p, o = own[core * CHIPS + j], sib[j]
        return jnp.where(core == first, p, o), jnp.where(core == first, o, p)

    def own_half(buf):
        return buf.at[pl.ds(core * CHIPS, CHIPS)]

    def other_half(buf):
        return buf.at[pl.ds((1 - core) * CHIPS, CHIPS)]

    def merge(own, sib, out, first):
        def go(j, carry):
            p, s = halves(own, sib, j, first)
            out[j, 0:32, :] = (s[32:33] * p[0:32] + s[0:32]).astype(BF16)
            decay = s[32:40] * p[32:40]
            decay = jnp.concatenate([decay, decay], axis=0)
            top = decay.astype(BF16).astype(F32)
            mid = (decay - top).astype(BF16).astype(F32)
            place = lax.broadcasted_iota(jnp.int32, (16, DH), 0)
            three = jnp.where(place < 5, top, jnp.where(place < 10, mid, decay - top - mid))
            out[j, 32:48, :] = three.astype(BF16)
            return carry

        lax.fori_loop(0, CHIPS, go, 0)

    def split(own, sib, got, out, out_sib, first):
        def go(j, carry):
            p, _ = halves(own, sib, j, first)
            early = got[j].astype(F32)
            late = p[32:33] * early + p[0:32]
            out[core * CHIPS + j] = jnp.where(core == first, early, late).astype(BF16)
            out_sib[j] = jnp.where(core == first, late, early).astype(BF16)
            return carry

        lax.fori_loop(0, CHIPS, go, 0)

    def a2a(n, src, dst, i, out):
        other = (chip + i) % CHIPS if out else (chip + CHIPS - i) % CHIPS
        return pltpu.make_async_remote_copy(
            src_ref=src.at[other], dst_ref=dst.at[chip if out else other],
            send_sem=a2a_s.at[n, i], recv_sem=a2a_r.at[n, i],
            device_id=(other * 2 + core, head, dp), device_id_type=pl.DeviceIdType.MESH,
        )

    def a2a_start(n, src, dst):
        def go(i, carry):
            a2a(n, src, dst, i, True).start()
            return carry

        lax.fori_loop(1, CHIPS, go, 0)
        dst[chip] = src[chip]

    def a2a_recv(n, src, dst):
        def go(i, carry):
            a2a(n, src, dst, i, False).wait_recv()
            return carry

        lax.fori_loop(1, CHIPS, go, 0)

    def a2a_sent(n, src, dst):
        def go(i, carry):
            a2a(n, src, dst, i, True).wait_send()
            return carry

        lax.fori_loop(1, CHIPS, go, 0)

    def scan(got, out, reverse):
        def go(i, state):
            at_chip = CHIPS - 1 - i if reverse else i
            out[at_chip] = state.astype(BF16)
            three = got[at_chip, 32:48, :].astype(F32)
            decay = three[0:1] + three[5:6] + three[10:11]
            return state * decay + got[at_chip, 0:32, :].astype(F32)

        lax.fori_loop(0, CHIPS, go, jnp.zeros((32, DH), F32))

    def state_of(buf, h):
        return buf[pl.ds(h * 4, 4)].reshape(DH, DH)

    heads(4, HEADS, fwd_share)
    send(("f", 0), other_half(cf), sf, dev_sib)
    step_a(0)
    recv(("f", 0), sf, dev_sib)
    merge(cf, sf, tf, 0)
    a2a_start(0, tf, rf)
    loads[4].wait()
    loads[5].wait()
    send(("go",), go_ref, go_sib, dev_sib)

    def inside(h, carry):
        scores = mm(q_ref[:, lanes(h)], k_ref[:, lanes(h)], NT)
        p = (scores * SCALE * weights(h)).astype(BF16)
        probs[h] = p
        intra[:, lanes(h)] = mm(p, v_ref[:, lanes(h)], NN)
        return carry

    heads(0, 2, inside)
    step_ao(0)
    step_z()
    step_b(0, 0)
    heads(2, 4, inside)
    step_b(0, 1)
    step_b(0, 2)
    a2a_recv(0, tf, rf)
    scan(rf, ef, False)
    a2a_start(1, ef, inf)
    step_a(1)
    heads(4, HEADS, inside)
    step_b(0, 3)
    sib_send(0, 1)
    sib_send(0, 2)
    step_ao(1)
    step_b(1, 0)

    a2a_recv(1, ef, inf)
    split(cf, sf, inf, low, lowf, 0)
    send(("f", 1), lowf, own_half(low), dev_sib)

    r = lax.broadcasted_iota(jnp.int32, (1024, DH), 0)
    place = r >> 4
    pc, pz, pb, pa = place >> 5, (place >> 4) & 1, (place >> 2) & 3, place & 3
    px = jnp.where(pc == 0, pa, pb)
    py = jnp.where(pc == 0, pb, pa)
    feature = 2 * ((((py * 4) + px) * 2 + pc) * 2 + pz) + ((r >> 3) & 1)
    lane = lax.broadcasted_iota(jnp.int32, (1024, DH), 1)
    same = feature == lane
    for h in range(HEADS):
        pt[:, h * DH : (h + 1) * DH] = jnp.where(same & ((r & 7) == h), 1.0, 0.0).astype(BF16)

    step_b(1, 1)
    step_b(1, 2)
    recv(("f", 1), other_half(low), dev_sib)

    def attend(h, carry):
        inter = mm(q_ref[:, lanes(h)], state_of(low, h), NN)
        factor = SCALE * jnp.exp(ccol[h])
        att[:, lanes(h)] = (intra[:, lanes(h)] + inter * factor).astype(BF16)
        return carry

    heads(0, HEADS, attend)
    step_b(1, 3)
    sib_send(1, 1)
    sib_send(1, 2)

    def turn(i, carry):
        rows = pl.ds(pl.multiple_of(i * 256, 256), 256)
        att_t[rows, :] = mm(pt[rows, :], att[...], NT).astype(BF16)
        attp[:, rows] = mm(att[...], pt[rows, :], NT).astype(BF16)
        return carry

    lax.fori_loop(0, 4, turn, 0)
    other_rows = pl.ds(pl.multiple_of((1 - core) * 512, 512), 512)
    send(("att",), att_t.at[other_rows], att_sib, dev_sib)
    for k in range(4):
        step_bo(0, k)
    sib_send(0, 3)

    recv(("go",), go_sib, dev_sib)
    recv(("att",), att_sib, dev_sib)
    lo, hi = pl.ds(0, HALF), pl.ds(HALF, HALF)

    def widen(ref):
        return ref.astype(F32)

    def rows_b(b1):
        return pl.ds(pl.multiple_of(b1 * 64, 64), 64)

    def rows_a(a1):
        return pl.ds(pl.multiple_of(a1 * 16, 16), 16)

    def w_block(zi):
        zz = (zo, z)[zi]
        own = pl.ds(pl.multiple_of(core * 512 + zz * 256, 256), 256)
        sib = pl.ds(pl.multiple_of(zz * 256, 256), 256)

        def go(n, carry):
            cols = pl.ds(pl.multiple_of(n * 256, 256), 256)
            value = mm(att_t[own, :], go_ref[:, cols], NN) + mm(att_sib[sib, :], go_sib[:, cols], NN)
            wp[zi, :, cols] = value.astype(BF16)
            return carry

        lax.fori_loop(0, 12, go, 0)

    def w_first(zi):
        w_block(zi)
        send(("w", zi, 0), wp.at[zi, rows_b(bo), lo], xb.at[zi, 0], dev_bp)
        send(("w", zi, 1), wp.at[zi, rows_b(bo), hi], xb.at[zi, 1], dev_bm)
        send(("w", zi, 2), wp.at[zi, rows_b(bp), hi], yb.at[zi, 0, :, hi], dev_bp)
        send(("w", zi, 3), wp.at[zi, rows_b(bm), lo], yb.at[zi, 1, :, lo], dev_bm)

    def w_relay(zi):
        recv(("w", zi, 0), xb.at[zi, 0], dev_bm)
        wp[zi, rows_b(bp), lo] = (widen(wp[zi, rows_b(bp), lo]) + widen(xb[zi, 0])).astype(BF16)
        send(("w", zi, 4), wp.at[zi, rows_b(bp), lo], yb.at[zi, 0, :, lo], dev_bp)
        recv(("w", zi, 1), xb.at[zi, 1], dev_bp)
        wp[zi, rows_b(bm), hi] = (widen(wp[zi, rows_b(bm), hi]) + widen(xb[zi, 1])).astype(BF16)
        send(("w", zi, 5), wp.at[zi, rows_b(bm), hi], yb.at[zi, 1, :, hi], dev_bm)

    def v_first(zi):
        recv(("w", zi, 2), yb.at[zi, 0, :, hi], dev_bm)
        recv(("w", zi, 3), yb.at[zi, 1, :, lo], dev_bp)
        recv(("w", zi, 4), yb.at[zi, 0, :, lo], dev_bm)
        recv(("w", zi, 5), yb.at[zi, 1, :, hi], dev_bp)

        def go(n, carry):
            cols = pl.ds(pl.multiple_of(n * 256, 256), 256)
            total = widen(wp[zi, rows_b(b), cols]) + widen(yb[zi, 0, :, cols]) + widen(yb[zi, 1, :, cols])
            wacc[zi, :, cols] = total
            wa[zi, :, cols] = total.astype(BF16)
            return carry

        lax.fori_loop(0, 12, go, 0)
        for n, (a1, dev) in enumerate(((ao, dev_ao), (ap, dev_ap), (am, dev_am))):
            send(("v", zi, n), wa.at[zi, rows_a(a1)], ya.at[zi, n], dev)

    def v_last(zi):
        for n, dev in enumerate((dev_ao, dev_am, dev_ap)):
            recv(("v", zi, n), ya.at[zi, n], dev)
        return wacc[zi, rows_a(a), :] + widen(ya[zi, 0]) + widen(ya[zi, 1]) + widen(ya[zi, 2])

    w_first(0)
    w_first(1)

    for k in range(4):
        step_bo(1, k)
    sib_send(1, 3)
    for zi in range(2):
        for k in range(4):
            sib_recv(zi, k)

    def mix(dest, store):
        def go(n, carry):
            cols = pl.ds(pl.multiple_of(dest * 768 + n * 256, 256), 256)
            w = panel[:, :, cols].reshape(1024, 256)
            store(pl.ds(pl.multiple_of(n * 256, 256), 256), mm(attp[...], w, NN))
            return carry

        lax.fori_loop(0, 3, go, 0)

    def store_at(dest):
        def store(cols, value):
            mp[dest, :, cols] = value.astype(BF16)

        return store

    def store_own(cols, value):
        macc[:, cols] = value

    mix(h3, store_at(h3))
    send(("m", 0), mp.at[h3], mr1.at[0], dev_h1)
    mix(h1, store_at(h1))
    send(("m", 1), mp.at[h1], mr1.at[1], dev_h1)

    def heads_grad(i, carry):
        rows = panel[pl.ds(i * 16, 16)].reshape(256, DOUT)
        cols = pl.ds(pl.multiple_of(i * 256, 256), 256)
        gh[:, cols] = mm(go_ref[...], rows, NT).astype(BF16)
        return carry

    lax.fori_loop(0, 4, heads_grad, 0)
    by_head = []
    for n in range(4):
        by_head.append(mm(gh[...], pt[:, n * 256 : (n + 1) * 256], NN).astype(BF16))
    for n in range(4):
        gh[:, n * 256 : (n + 1) * 256] = by_head[n]

    def bwd_share(h, carry):
        qw = (q_ref[:, lanes(h)].astype(F32) * (SCALE * jnp.exp(ccol[h]))).astype(BF16)
        last = ccol[h, BLOCK - 1 : BLOCK, :]
        pieces(cb, h, mm(qw, gh[:, lanes(h)], TN), jnp.exp(last))
        return carry

    heads(0, HEADS, bwd_share)
    send(("k", 0), other_half(cb), sb, dev_sib)
    w_relay(0)
    recv(("k", 0), sb, dev_sib)
    merge(cb, sb, tb, 1)
    a2a_start(2, tb, rb)
    w_relay(1)
    mix(h2, store_at(h2))

    def grads(h, carry):
        g, kk, vv, qq = gh[:, lanes(h)], k_ref[:, lanes(h)], v_ref[:, lanes(h)], q_ref[:, lanes(h)]
        dp_h = (mm(g, vv, NT) * SCALE * weights(h)).astype(BF16)
        factor = SCALE * jnp.exp(ccol[h])
        qg = mm(dp_h, kk, NN) + mm(g, state_of(low, h), NT) * factor
        qg_ref[:, lanes(h)] = qg.astype(BF16)
        kpart[:, lanes(h)] = mm(dp_h, qq, TN)
        vpart[:, lanes(h)] = mm(probs[h], g, TN)
        return carry

    heads(0, 2, grads)
    v_first(0)
    recv(("m", 0), mr1.at[0], dev_h1)
    mp[h2] = (widen(mp[h2]) + widen(mr1[0])).astype(BF16)
    send(("m", 2), mp.at[h2], mr2, dev_h2)
    a2a_recv(2, tb, rb)
    scan(rb, eb, True)
    a2a_start(3, eb, inb)
    heads(2, 4, grads)
    v_first(1)
    heads(4, HEADS, grads)
    wa[0, rows_a(a), :] = v_last(0).astype(BF16)
    send(("vz",), wa.at[0, rows_a(a)], xz, dev_z)

    a2a_recv(3, eb, inb)
    split(cb, sb, inb, back, lowb, 1)
    send(("k", 1), lowb, own_half(back), dev_sib)
    outs = [
        pltpu.make_async_copy(src, dst, osem.at[i])
        for i, (src, dst) in enumerate(
            ((qg_ref, qg_out), (kg_ref, kg_out), (vg_ref, vg_out), (mixed_ref, mixed_out), (wg_ref, wg_out))
        )
    ]
    outs[0].start()
    mix(head, store_own)
    recv(("k", 1), other_half(back), dev_sib)

    def finish(h, carry):
        col = ccol[h]
        tail = jnp.exp(col[BLOCK - 1 : BLOCK, :] - col)
        state = state_of(back, h)
        kg = kpart[:, lanes(h)] + tail * mm(v_ref[:, lanes(h)], state, NT)
        vg = vpart[:, lanes(h)] + tail * mm(k_ref[:, lanes(h)], state, NN)
        kg_ref[:, lanes(h)] = kg.astype(BF16)
        vg_ref[:, lanes(h)] = vg.astype(BF16)
        return carry

    heads(0, HEADS, finish)
    outs[1].start()
    outs[2].start()

    wg_ref[...] = v_last(1)
    recv(("vz",), xz, dev_z)
    wg_ref[...] += widen(xz[...])
    outs[4].start()

    recv(("m", 1), mr1.at[1], dev_h1)
    recv(("m", 2), mr2, dev_h2)
    mixed_ref[...] = (macc[...] + widen(mr1[1]) + widen(mr2[...])).astype(BF16)
    outs[3].start()

    for copy in started:
        copy.wait_send()
    for n, src, dst in ((0, tf, rf), (1, ef, inf), (2, tb, rb), (3, eb, inb)):
        a2a_sent(n, src, dst)
    for out in outs:
        out.wait()


def hand_out(*refs):
    n = len(refs) // 3
    given, out, held, sems = refs[:n], refs[n : 2 * n], refs[2 * n : 3 * n], refs[-1]
    first = [pltpu.make_async_copy(given[i], held[i], sems.at[0, i]) for i in range(n)]
    second = [pltpu.make_async_copy(held[i], out[i], sems.at[1, i]) for i in range(n)]
    for copy in first:
        copy.start()
    for i in range(n):
        first[i].wait()
        second[i].start()
    for copy in second:
        copy.wait()


def shards(queries, keys, values, log_decay, w_out, grad_out):
    hbm = pl.BlockSpec(memory_space=pl.ANY)
    length = queries.shape[1]
    features = HEADS * DH
    shapes = (
        jax.ShapeDtypeStruct((length, DOUT // 4), BF16),
        jax.ShapeDtypeStruct((length, features), BF16),
        jax.ShapeDtypeStruct((length, features), BF16),
        jax.ShapeDtypeStruct((length, features), BF16),
        jax.ShapeDtypeStruct((16, DOUT), F32),
    )
    whole = pltpu.VMEM((length, features), BF16)
    wide = pltpu.VMEM((length, features), F32)
    piece = pltpu.VMEM((CHIPS, 48, DH), BF16)
    state = pltpu.VMEM((CHIPS, 32, DH), BF16)
    scan = [
        pltpu.VMEM((2 * CHIPS, 40, DH), F32), pltpu.VMEM((CHIPS, 40, DH), F32), piece, piece,
        state, state, state, pltpu.VMEM((2 * CHIPS, 32, DH), BF16),
    ]

    results = pl.pallas_call(
        kernel,
        out_shape=shapes,
        in_specs=[hbm] * 6,
        out_specs=(hbm,) * 5,
        scratch_shapes=[
            whole,
            whole,
            whole,
            pltpu.VMEM((HEADS, BLOCK), F32),
            pltpu.VMEM((BLOCK, DOUT), BF16),
            pltpu.VMEM((BLOCK, DOUT // 4), BF16),
            whole,
            whole,
            whole,
            pltpu.VMEM((16, DOUT), F32),
            pltpu.VMEM((64, 16, DOUT), BF16),
            pltpu.VMEM((features, features), BF16),
            pltpu.VMEM((HEADS, BLOCK), F32),
            pltpu.VMEM((HEADS, BLOCK, DH), F32),
            pltpu.VMEM((HEADS, BLOCK, BLOCK), BF16),
            wide,
            wide,
            wide,
            whole,
            whole,
            whole,
            *scan,
            *scan,
            pltpu.VMEM((BLOCK, DOUT), BF16),
            pltpu.VMEM((features, BLOCK), BF16),
            pltpu.VMEM((512, BLOCK), BF16),
            pltpu.VMEM((2, 256, DOUT), BF16),
            pltpu.VMEM((2, 2, 64, HALF), BF16),
            pltpu.VMEM((2, 2, 64, DOUT), BF16),
            pltpu.VMEM((2, 64, DOUT), F32),
            pltpu.VMEM((2, 64, DOUT), BF16),
            pltpu.VMEM((2, 3, 16, DOUT), BF16),
            pltpu.VMEM((16, DOUT), BF16),
            pltpu.VMEM((4, BLOCK, 768), BF16),
            pltpu.VMEM((BLOCK, 768), F32),
            pltpu.VMEM((2, BLOCK, 768), BF16),
            pltpu.VMEM((BLOCK, 768), BF16),
            pltpu.SemaphoreType.DMA((88,)),
            pltpu.SemaphoreType.DMA((88,)),
            pltpu.SemaphoreType.DMA((4, CHIPS)),
            pltpu.SemaphoreType.DMA((4, CHIPS)),
            pltpu.SemaphoreType.DMA((6,)),
            pltpu.SemaphoreType.DMA((5,)),
        ],
        compiler_params=pltpu.CompilerParams(
            collective_id=0, has_side_effects=True, vmem_limit_bytes=60 * 1024 * 1024
        ),
        name="step",
    )(queries[0], keys[0], values[0], log_decay[0], w_out.reshape(16, DOUT), grad_out[0])
    mixed, qg, kg, vg, wg = pl.pallas_call(
        hand_out,
        out_shape=shapes,
        in_specs=[hbm] * 5,
        out_specs=(hbm,) * 5,
        scratch_shapes=[*(pltpu.VMEM(s.shape, s.dtype) for s in shapes), pltpu.SemaphoreType.DMA((2, 5))],
        compiler_params=pltpu.CompilerParams(vmem_limit_bytes=60 * 1024 * 1024),
        name="hand_out",
    )(*results)
    return mixed[None], qg[None], kg[None], vg[None], wg.reshape(2, HEADS, DOUT)


def solution(mesh):
    return jax.shard_map(
        shards,
        mesh=mesh,
        in_specs=(
            P("dp", "ctx", "head"),
            P("dp", "ctx", "head"),
            P("dp", "ctx", "head"),
            P("dp", "head", "ctx"),
            P(("ctx", "dp"), "head", None),
            P("dp", "ctx", None),
        ),
        out_specs=(
            P("dp", "ctx", "head"),
            P("dp", "ctx", "head"),
            P("dp", "ctx", "head"),
            P("dp", "ctx", "head"),
            P(("ctx", "dp"), "head", None),
        ),
        check_vma=False,
    )
```

```python
import jax
import jax.numpy as jnp
from jax import lax
from jax.experimental import pallas as pl
from jax.experimental.pallas import tpu as pltpu
from jax.sharding import PartitionSpec as P

DH = 128
BLOCK = 256
HEADS = 8
DOUT = 3072
HALF = DOUT // 2
CHIPS = 16
SCALE = 1.0 / DH
F32 = jnp.float32
BF16 = jnp.bfloat16
NT = (((1,), (1,)), ((), ()))
NN = (((1,), (0,)), ((), ()))
TN = (((0,), (0,)), ((), ()))


def mm(a, b, dims):
    return lax.dot_general(a, b, dims, preferred_element_type=F32)


class Ids:
    def __init__(self):
        self.names = {}

    def __call__(self, *name):
        return self.names.setdefault(name, len(self.names))


def kernel(
    q_in, k_in, v_in, ld_in, w_in, go_in,
    mixed_out, qg_out, kg_out, vg_out, wg_out,
    q_ref, k_ref, v_ref, ld_ref, go_ref, mixed_ref, qg_ref, kg_ref, vg_ref, wg_ref,
    panel, pt, cum, ccol, probs, intra, kpart, vpart, att, attp, gh,
    cf, sf, tf, rf, ef, inf, lowf, low, cb, sb, tb, rb, eb, inb, lowb, back,
    go_sib, att_t, att_sib,
    wp, xb, yb, wacc, wa, ya, xz,
    mp, macc, mr1, mr2,
    ssem, rsem, a2a_s, a2a_r, isem, osem,
):
    ctx, head, dp = lax.axis_index("ctx"), lax.axis_index("head"), lax.axis_index("dp")
    core, chip = ctx % 2, ctx // 2
    x, y = chip % 4, ctx // 8
    a = x * (1 - core) + y * core
    b = y * (1 - core) + x * core
    ap, am, ao = (a + 1) % 4, (a + 3) % 4, (a + 2) % 4
    bp, bm, bo = (b + 1) % 4, (b + 3) % 4, (b + 2) % 4
    z, zo = dp, 1 - dp

    def at(a1, b1):
        x1 = a1 * (1 - core) + b1 * core
        y1 = b1 * (1 - core) + a1 * core
        return ((y1 * 4 + x1) * 2 + core, head, dp)

    dev_ap, dev_am, dev_ao, dev_bp, dev_bm = at(ap, b), at(am, b), at(ao, b), at(a, bp), at(a, bm)
    dev_sib = (ctx + 1 - 2 * core, head, dp)
    dev_z = (ctx, head, zo)
    h1 = head + 1 - 2 * (head % 2)
    h2 = (head + 2) % 4
    h3 = (h1 + 2) % 4
    dev_h1, dev_h2 = (ctx, h1, dp), (ctx, h2, dp)

    ids = Ids()
    started = []

    def xfer(name, src, dst, dev):
        i = ids(*name)
        return pltpu.make_async_remote_copy(
            src_ref=src, dst_ref=dst, send_sem=ssem.at[i], recv_sem=rsem.at[i],
            device_id=dev, device_id_type=pl.DeviceIdType.MESH,
        )

    def send(name, src, dst, dev):
        copy = xfer(name, src, dst, dev)
        copy.start()
        started.append(copy)

    def recv(name, ref, dev):
        xfer(name, ref, ref, dev).wait_recv()

    def slot(a1, b1, z1):
        return core * 32 + z1 * 16 + b1 * 4 + a1

    mine = slot(a, b, z)
    pairs = ((w_in, panel.at[mine]), (ld_in, ld_ref), (k_in, k_ref), (v_in, v_ref), (q_in, q_ref), (go_in, go_ref))
    loads = [pltpu.make_async_copy(src, dst, isem.at[i]) for i, (src, dst) in enumerate(pairs)]
    for load in loads:
        load.start()

    barrier = pltpu.get_barrier_semaphore()

    def greet(i, carry):
        pl.semaphore_signal(
            barrier, inc=1, device_id=((chip + i) % CHIPS * 2 + core, head, dp), device_id_type=pl.DeviceIdType.MESH
        )
        return carry

    lax.fori_loop(1, CHIPS, greet, 0)
    for dev in (dev_sib, dev_z, dev_h1, dev_h2):
        pl.semaphore_signal(barrier, inc=1, device_id=dev, device_id_type=pl.DeviceIdType.MESH)
    for load in loads[1:4]:
        load.wait()

    t_row = lax.broadcasted_iota(jnp.int32, (BLOCK, BLOCK), 0)
    t_col = lax.broadcasted_iota(jnp.int32, (BLOCK, BLOCK), 1)
    upper = (t_row <= t_col).astype(F32)
    cum[...] = jnp.dot(ld_ref[...], upper, precision=lax.Precision.HIGHEST, preferred_element_type=F32)

    def heads(first, last, body):
        lax.fori_loop(first, last, body, 0, unroll=2 if (last - first) % 2 == 0 else 1)

    def lanes(h):
        return pl.ds(pl.multiple_of(h * DH, DH), DH)

    def pieces(buf, h, total, decay):
        for r in range(4):
            buf[h * 4 + r, 0:32, :] = total[r * 32 : (r + 1) * 32]
            buf[h * 4 + r, 32:40, :] = jnp.broadcast_to(decay, (8, DH))

    def fwd_share(h, carry):
        wide = jnp.broadcast_to(cum[pl.ds(h, 1), :], (DH, BLOCK))
        col = wide.T
        ccol[h] = col
        last = col[BLOCK - 1 : BLOCK, :]
        kw = (k_ref[:, lanes(h)].astype(F32) * jnp.exp(last - col)).astype(BF16)
        pieces(cf, h, mm(kw, v_ref[:, lanes(h)], TN), jnp.exp(last))
        return carry

    heads(0, 4, fwd_share)
    pl.semaphore_wait(barrier, CHIPS - 1 + 4)

    def whole(s):
        return panel.at[s]

    def part(s, h):
        return panel.at[s, :, pl.ds(h * HALF, HALF)]

    a_of = {0: a, 1: am, 2: ap, 3: ao}

    def b_sends(zi, k):
        zz = (z, zo)[zi]
        ref = whole(slot(a_of[k], b, zz))
        send(("bp", zi, k), ref, ref, dev_bp)
        send(("bm", zi, k), ref, ref, dev_bm)

    def a_sends(zi):
        ref = whole(slot(a, b, (z, zo)[zi]))
        send(("ap", zi), ref, ref, dev_ap)
        send(("am", zi), ref, ref, dev_am)
        send(("ao", zi), ref, ref, dev_ao)

    def step_a(zi):
        zz = (z, zo)[zi]
        left, right = slot(am, b, zz), slot(ap, b, zz)
        recv(("ap", zi), whole(left), dev_am)
        b_sends(zi, 1)
        recv(("am", zi), whole(right), dev_ap)
        b_sends(zi, 2)

    def step_ao(zi):
        far = slot(ao, b, (z, zo)[zi])
        recv(("ao", zi), whole(far), dev_ao)
        b_sends(zi, 3)
        sib_send(zi, 0)

    def step_b(zi, k):
        zz = (z, zo)[zi]
        below, above = slot(a_of[k], bm, zz), slot(a_of[k], bp, zz)
        recv(("bp", zi, k), whole(below), dev_bm)
        send(("bfp", zi, k), part(below, 0), part(below, 0), dev_bp)
        recv(("bm", zi, k), whole(above), dev_bp)
        send(("bfm", zi, k), part(above, 1), part(above, 1), dev_bm)

    def step_bo(zi, k):
        far = slot(a_of[k], bo, (z, zo)[zi])
        recv(("bfp", zi, k), part(far, 0), dev_bm)
        recv(("bfm", zi, k), part(far, 1), dev_bp)

    def step_z():
        recv(("z",), whole(slot(a, b, zo)), dev_z)
        a_sends(1)
        b_sends(1, 0)

    def row(c1, b1, z1):
        return panel.at[pl.ds(c1 * 32 + z1 * 16 + b1 * 4, 4)]

    def sib_send(zi, k):
        ref = row(core, (b, bm, bp, bo)[k], (z, zo)[zi])
        send(("sib", zi, k), ref, ref, dev_sib)

    def sib_recv(zi, k):
        recv(("sib", zi, k), row(1 - core, (a, am, ap, ao)[k], (z, zo)[zi]), dev_sib)

    loads[0].wait()
    send(("z",), whole(mine), whole(mine), dev_z)
    a_sends(0)
    b_sends(0, 0)
    def weights(h):
        col = ccol[h]
        spread = jnp.concatenate([col, col], axis=1) - cum[pl.ds(h, 1), :]
        rows = lax.broadcasted_iota(jnp.int32, (BLOCK, BLOCK), 0)
        cols = lax.broadcasted_iota(jnp.int32, (BLOCK, BLOCK), 1)
        return jnp.exp(jnp.where(rows >= cols, spread, -jnp.inf))

    def halves(own, sib, j, first):
        p, o = own[core * CHIPS + j], sib[j]
        return jnp.where(core == first, p, o), jnp.where(core == first, o, p)

    def own_half(buf):
        return buf.at[pl.ds(core * CHIPS, CHIPS)]

    def other_half(buf):
        return buf.at[pl.ds((1 - core) * CHIPS, CHIPS)]

    def merge(own, sib, out, first):
        def go(j, carry):
            p, s = halves(own, sib, j, first)
            out[j, 0:32, :] = (s[32:33] * p[0:32] + s[0:32]).astype(BF16)
            decay = s[32:40] * p[32:40]
            decay = jnp.concatenate([decay, decay], axis=0)
            top = decay.astype(BF16).astype(F32)
            mid = (decay - top).astype(BF16).astype(F32)
            place = lax.broadcasted_iota(jnp.int32, (16, DH), 0)
            three = jnp.where(place < 5, top, jnp.where(place < 10, mid, decay - top - mid))
            out[j, 32:48, :] = three.astype(BF16)
            return carry

        lax.fori_loop(0, CHIPS, go, 0, unroll=2)

    def split(own, sib, got, out, out_sib, first):
        def go(j, carry):
            p, _ = halves(own, sib, j, first)
            early = got[j].astype(F32)
            late = p[32:33] * early + p[0:32]
            out[core * CHIPS + j] = jnp.where(core == first, early, late).astype(BF16)
            out_sib[j] = jnp.where(core == first, late, early).astype(BF16)
            return carry

        lax.fori_loop(0, CHIPS, go, 0, unroll=2)

    def a2a(n, src, dst, i, out):
        other = (chip + i) % CHIPS if out else (chip + CHIPS - i) % CHIPS
        return pltpu.make_async_remote_copy(
            src_ref=src.at[other], dst_ref=dst.at[chip if out else other],
            send_sem=a2a_s.at[n, i], recv_sem=a2a_r.at[n, i],
            device_id=(other * 2 + core, head, dp), device_id_type=pl.DeviceIdType.MESH,
        )

    def a2a_start(n, src, dst):
        def go(i, carry):
            a2a(n, src, dst, i, True).start()
            return carry

        lax.fori_loop(1, CHIPS, go, 0)
        dst[chip] = src[chip]

    def a2a_recv(n, src, dst):
        def go(i, carry):
            a2a(n, src, dst, i, False).wait_recv()
            return carry

        lax.fori_loop(1, CHIPS, go, 0)

    def a2a_sent(n, src, dst):
        def go(i, carry):
            a2a(n, src, dst, i, True).wait_send()
            return carry

        lax.fori_loop(1, CHIPS, go, 0)

    def scan(got, out, reverse):
        def go(i, state):
            at_chip = CHIPS - 1 - i if reverse else i
            out[at_chip] = state.astype(BF16)
            three = got[at_chip, 32:48, :].astype(F32)
            decay = three[0:1] + three[5:6] + three[10:11]
            return state * decay + got[at_chip, 0:32, :].astype(F32)

        lax.fori_loop(0, CHIPS, go, jnp.zeros((32, DH), F32), unroll=2)

    def state_of(buf, h):
        return buf[pl.ds(h * 4, 4)].reshape(DH, DH)

    heads(4, HEADS, fwd_share)
    send(("f", 0), other_half(cf), sf, dev_sib)
    step_a(0)
    recv(("f", 0), sf, dev_sib)
    merge(cf, sf, tf, 0)
    a2a_start(0, tf, rf)
    loads[4].wait()
    loads[5].wait()
    send(("go",), go_ref, go_sib, dev_sib)

    def inside(h, carry):
        scores = mm(q_ref[:, lanes(h)], k_ref[:, lanes(h)], NT)
        p = (scores * SCALE * weights(h)).astype(BF16)
        probs[h] = p
        intra[:, lanes(h)] = mm(p, v_ref[:, lanes(h)], NN)
        return carry

    heads(0, 2, inside)
    step_ao(0)
    step_z()
    step_b(0, 0)
    heads(2, 4, inside)
    step_b(0, 1)
    step_b(0, 2)
    a2a_recv(0, tf, rf)
    scan(rf, ef, False)
    a2a_start(1, ef, inf)
    step_a(1)
    heads(4, HEADS, inside)
    step_b(0, 3)
    sib_send(0, 1)
    sib_send(0, 2)
    step_ao(1)
    step_b(1, 0)

    a2a_recv(1, ef, inf)
    split(cf, sf, inf, low, lowf, 0)
    send(("f", 1), lowf, own_half(low), dev_sib)

    r = lax.broadcasted_iota(jnp.int32, (1024, DH), 0)
    place = r >> 4
    pc, pz, pb, pa = place >> 5, (place >> 4) & 1, (place >> 2) & 3, place & 3
    px = jnp.where(pc == 0, pa, pb)
    py = jnp.where(pc == 0, pb, pa)
    feature = 2 * ((((py * 4) + px) * 2 + pc) * 2 + pz) + ((r >> 3) & 1)
    lane = lax.broadcasted_iota(jnp.int32, (1024, DH), 1)
    same = feature == lane
    for h in range(HEADS):
        pt[:, h * DH : (h + 1) * DH] = jnp.where(same & ((r & 7) == h), 1.0, 0.0).astype(BF16)

    step_b(1, 1)
    step_b(1, 2)
    recv(("f", 1), other_half(low), dev_sib)

    def attend(h, carry):
        inter = mm(q_ref[:, lanes(h)], state_of(low, h), NN)
        factor = SCALE * jnp.exp(ccol[h])
        att[:, lanes(h)] = (intra[:, lanes(h)] + inter * factor).astype(BF16)
        return carry

    heads(0, HEADS, attend)
    step_b(1, 3)
    sib_send(1, 1)
    sib_send(1, 2)

    def turn(i, carry):
        rows = pl.ds(pl.multiple_of(i * 256, 256), 256)
        att_t[rows, :] = mm(pt[rows, :], att[...], NT).astype(BF16)
        attp[:, rows] = mm(att[...], pt[rows, :], NT).astype(BF16)
        return carry

    lax.fori_loop(0, 4, turn, 0, unroll=2)
    other_rows = pl.ds(pl.multiple_of((1 - core) * 512, 512), 512)
    send(("att",), att_t.at[other_rows], att_sib, dev_sib)
    for k in range(4):
        step_bo(0, k)
    sib_send(0, 3)

    recv(("go",), go_sib, dev_sib)
    recv(("att",), att_sib, dev_sib)
    lo, hi = pl.ds(0, HALF), pl.ds(HALF, HALF)

    def widen(ref):
        return ref.astype(F32)

    def rows_b(b1):
        return pl.ds(pl.multiple_of(b1 * 64, 64), 64)

    def rows_a(a1):
        return pl.ds(pl.multiple_of(a1 * 16, 16), 16)

    def w_block(zi):
        zz = (zo, z)[zi]
        own = pl.ds(pl.multiple_of(core * 512 + zz * 256, 256), 256)
        sib = pl.ds(pl.multiple_of(zz * 256, 256), 256)

        def go(n, carry):
            cols = pl.ds(pl.multiple_of(n * 256, 256), 256)
            value = mm(att_t[own, :], go_ref[:, cols], NN) + mm(att_sib[sib, :], go_sib[:, cols], NN)
            wp[zi, :, cols] = value.astype(BF16)
            return carry

        lax.fori_loop(0, 12, go, 0, unroll=2)

    def w_first(zi):
        w_block(zi)
        send(("w", zi, 0), wp.at[zi, rows_b(bo), lo], xb.at[zi, 0], dev_bp)
        send(("w", zi, 1), wp.at[zi, rows_b(bo), hi], xb.at[zi, 1], dev_bm)
        send(("w", zi, 2), wp.at[zi, rows_b(bp), hi], yb.at[zi, 0, :, hi], dev_bp)
        send(("w", zi, 3), wp.at[zi, rows_b(bm), lo], yb.at[zi, 1, :, lo], dev_bm)

    def w_relay(zi):
        recv(("w", zi, 0), xb.at[zi, 0], dev_bm)
        wp[zi, rows_b(bp), lo] = (widen(wp[zi, rows_b(bp), lo]) + widen(xb[zi, 0])).astype(BF16)
        send(("w", zi, 4), wp.at[zi, rows_b(bp), lo], yb.at[zi, 0, :, lo], dev_bp)
        recv(("w", zi, 1), xb.at[zi, 1], dev_bp)
        wp[zi, rows_b(bm), hi] = (widen(wp[zi, rows_b(bm), hi]) + widen(xb[zi, 1])).astype(BF16)
        send(("w", zi, 5), wp.at[zi, rows_b(bm), hi], yb.at[zi, 1, :, hi], dev_bm)

    def v_first(zi):
        recv(("w", zi, 2), yb.at[zi, 0, :, hi], dev_bm)
        recv(("w", zi, 3), yb.at[zi, 1, :, lo], dev_bp)
        recv(("w", zi, 4), yb.at[zi, 0, :, lo], dev_bm)
        recv(("w", zi, 5), yb.at[zi, 1, :, hi], dev_bp)

        def go(n, carry):
            cols = pl.ds(pl.multiple_of(n * 256, 256), 256)
            total = widen(wp[zi, rows_b(b), cols]) + widen(yb[zi, 0, :, cols]) + widen(yb[zi, 1, :, cols])
            wacc[zi, :, cols] = total
            wa[zi, :, cols] = total.astype(BF16)
            return carry

        lax.fori_loop(0, 12, go, 0, unroll=2)
        for n, (a1, dev) in enumerate(((ao, dev_ao), (ap, dev_ap), (am, dev_am))):
            send(("v", zi, n), wa.at[zi, rows_a(a1)], ya.at[zi, n], dev)

    def v_last(zi):
        for n, dev in enumerate((dev_ao, dev_am, dev_ap)):
            recv(("v", zi, n), ya.at[zi, n], dev)
        return wacc[zi, rows_a(a), :] + widen(ya[zi, 0]) + widen(ya[zi, 1]) + widen(ya[zi, 2])

    w_first(0)
    for k in range(4):
        step_bo(1, k)
    sib_send(1, 3)
    w_first(1)
    for zi in range(2):
        for k in range(4):
            sib_recv(zi, k)

    def mix(dest, store):
        def go(n, carry):
            cols = pl.ds(pl.multiple_of(dest * 768 + n * 256, 256), 256)
            w = panel[:, :, cols].reshape(1024, 256)
            store(pl.ds(pl.multiple_of(n * 256, 256), 256), mm(attp[...], w, NN))
            return carry

        lax.fori_loop(0, 3, go, 0, unroll=3)

    def store_at(dest):
        def store(cols, value):
            mp[dest, :, cols] = value.astype(BF16)

        return store

    def store_own(cols, value):
        macc[:, cols] = value

    mix(h3, store_at(h3))
    send(("m", 0), mp.at[h3], mr1.at[0], dev_h1)
    mix(h1, store_at(h1))
    send(("m", 1), mp.at[h1], mr1.at[1], dev_h1)

    def heads_grad(i, carry):
        rows = panel[pl.ds(i * 16, 16)].reshape(256, DOUT)
        cols = pl.ds(pl.multiple_of(i * 256, 256), 256)
        gh[:, cols] = mm(go_ref[...], rows, NT).astype(BF16)
        return carry

    lax.fori_loop(0, 4, heads_grad, 0, unroll=2)
    by_head = []
    for n in range(4):
        by_head.append(mm(gh[...], pt[:, n * 256 : (n + 1) * 256], NN).astype(BF16))
    for n in range(4):
        gh[:, n * 256 : (n + 1) * 256] = by_head[n]

    def bwd_share(h, carry):
        qw = (q_ref[:, lanes(h)].astype(F32) * (SCALE * jnp.exp(ccol[h]))).astype(BF16)
        last = ccol[h, BLOCK - 1 : BLOCK, :]
        pieces(cb, h, mm(qw, gh[:, lanes(h)], TN), jnp.exp(last))
        return carry

    heads(0, HEADS, bwd_share)
    send(("k", 0), other_half(cb), sb, dev_sib)
    w_relay(0)
    recv(("k", 0), sb, dev_sib)
    merge(cb, sb, tb, 1)
    a2a_start(2, tb, rb)
    w_relay(1)
    mix(h2, store_at(h2))

    def grads(h, carry):
        g, kk, vv, qq = gh[:, lanes(h)], k_ref[:, lanes(h)], v_ref[:, lanes(h)], q_ref[:, lanes(h)]
        dp_h = (mm(g, vv, NT) * SCALE * weights(h)).astype(BF16)
        factor = SCALE * jnp.exp(ccol[h])
        qg = mm(dp_h, kk, NN) + mm(g, state_of(low, h), NT) * factor
        qg_ref[:, lanes(h)] = qg.astype(BF16)
        kpart[:, lanes(h)] = mm(dp_h, qq, TN)
        vpart[:, lanes(h)] = mm(probs[h], g, TN)
        return carry

    heads(0, 2, grads)
    v_first(0)
    recv(("m", 0), mr1.at[0], dev_h1)
    mp[h2] = (widen(mp[h2]) + widen(mr1[0])).astype(BF16)
    send(("m", 2), mp.at[h2], mr2, dev_h2)
    a2a_recv(2, tb, rb)
    scan(rb, eb, True)
    a2a_start(3, eb, inb)
    heads(2, 4, grads)
    v_first(1)
    heads(4, HEADS, grads)
    wa[0, rows_a(a), :] = v_last(0).astype(BF16)
    send(("vz",), wa.at[0, rows_a(a)], xz, dev_z)

    a2a_recv(3, eb, inb)
    split(cb, sb, inb, back, lowb, 1)
    send(("k", 1), lowb, own_half(back), dev_sib)
    outs = [
        pltpu.make_async_copy(src, dst, osem.at[i])
        for i, (src, dst) in enumerate(
            ((qg_ref, qg_out), (kg_ref, kg_out), (vg_ref, vg_out), (mixed_ref, mixed_out), (wg_ref, wg_out))
        )
    ]
    outs[0].start()
    mix(head, store_own)
    recv(("k", 1), other_half(back), dev_sib)

    def finish(h, carry):
        col = ccol[h]
        tail = jnp.exp(col[BLOCK - 1 : BLOCK, :] - col)
        state = state_of(back, h)
        kg = kpart[:, lanes(h)] + tail * mm(v_ref[:, lanes(h)], state, NT)
        vg = vpart[:, lanes(h)] + tail * mm(k_ref[:, lanes(h)], state, NN)
        kg_ref[:, lanes(h)] = kg.astype(BF16)
        vg_ref[:, lanes(h)] = vg.astype(BF16)
        return carry

    heads(0, HEADS, finish)
    outs[1].start()
    outs[2].start()

    wg_ref[...] = v_last(1)
    recv(("vz",), xz, dev_z)
    wg_ref[...] += widen(xz[...])
    outs[4].start()

    recv(("m", 1), mr1.at[1], dev_h1)
    recv(("m", 2), mr2, dev_h2)
    mixed_ref[...] = (macc[...] + widen(mr1[1]) + widen(mr2[...])).astype(BF16)
    outs[3].start()

    for copy in started:
        copy.wait_send()
    for n, src, dst in ((0, tf, rf), (1, ef, inf), (2, tb, rb), (3, eb, inb)):
        a2a_sent(n, src, dst)
    for out in outs:
        out.wait()


def hand_out(*refs):
    n = len(refs) // 3
    given, out, held, sems = refs[:n], refs[n : 2 * n], refs[2 * n : 3 * n], refs[-1]
    first = [pltpu.make_async_copy(given[i], held[i], sems.at[0, i]) for i in range(n)]
    second = [pltpu.make_async_copy(held[i], out[i], sems.at[1, i]) for i in range(n)]
    for copy in first:
        copy.start()
    for i in range(n):
        first[i].wait()
        second[i].start()
    for copy in second:
        copy.wait()


def shards(queries, keys, values, log_decay, w_out, grad_out):
    hbm = pl.BlockSpec(memory_space=pl.ANY)
    length = queries.shape[1]
    features = HEADS * DH
    shapes = (
        jax.ShapeDtypeStruct((length, DOUT // 4), BF16),
        jax.ShapeDtypeStruct((length, features), BF16),
        jax.ShapeDtypeStruct((length, features), BF16),
        jax.ShapeDtypeStruct((length, features), BF16),
        jax.ShapeDtypeStruct((16, DOUT), F32),
    )
    whole = pltpu.VMEM((length, features), BF16)
    wide = pltpu.VMEM((length, features), F32)
    piece = pltpu.VMEM((CHIPS, 48, DH), BF16)
    state = pltpu.VMEM((CHIPS, 32, DH), BF16)
    scan = [
        pltpu.VMEM((2 * CHIPS, 40, DH), F32), pltpu.VMEM((CHIPS, 40, DH), F32), piece, piece,
        state, state, state, pltpu.VMEM((2 * CHIPS, 32, DH), BF16),
    ]

    results = pl.pallas_call(
        kernel,
        out_shape=shapes,
        in_specs=[hbm] * 6,
        out_specs=(hbm,) * 5,
        scratch_shapes=[
            whole,
            whole,
            whole,
            pltpu.VMEM((HEADS, BLOCK), F32),
            pltpu.VMEM((BLOCK, DOUT), BF16),
            pltpu.VMEM((BLOCK, DOUT // 4), BF16),
            whole,
            whole,
            whole,
            pltpu.VMEM((16, DOUT), F32),
            pltpu.VMEM((64, 16, DOUT), BF16),
            pltpu.VMEM((features, features), BF16),
            pltpu.VMEM((HEADS, BLOCK), F32),
            pltpu.VMEM((HEADS, BLOCK, DH), F32),
            pltpu.VMEM((HEADS, BLOCK, BLOCK), BF16),
            wide,
            wide,
            wide,
            whole,
            whole,
            whole,
            *scan,
            *scan,
            pltpu.VMEM((BLOCK, DOUT), BF16),
            pltpu.VMEM((features, BLOCK), BF16),
            pltpu.VMEM((512, BLOCK), BF16),
            pltpu.VMEM((2, 256, DOUT), BF16),
            pltpu.VMEM((2, 2, 64, HALF), BF16),
            pltpu.VMEM((2, 2, 64, DOUT), BF16),
            pltpu.VMEM((2, 64, DOUT), F32),
            pltpu.VMEM((2, 64, DOUT), BF16),
            pltpu.VMEM((2, 3, 16, DOUT), BF16),
            pltpu.VMEM((16, DOUT), BF16),
            pltpu.VMEM((4, BLOCK, 768), BF16),
            pltpu.VMEM((BLOCK, 768), F32),
            pltpu.VMEM((2, BLOCK, 768), BF16),
            pltpu.VMEM((BLOCK, 768), BF16),
            pltpu.SemaphoreType.DMA((88,)),
            pltpu.SemaphoreType.DMA((88,)),
            pltpu.SemaphoreType.DMA((4, CHIPS)),
            pltpu.SemaphoreType.DMA((4, CHIPS)),
            pltpu.SemaphoreType.DMA((6,)),
            pltpu.SemaphoreType.DMA((5,)),
        ],
        compiler_params=pltpu.CompilerParams(
            collective_id=0, has_side_effects=True, vmem_limit_bytes=60 * 1024 * 1024
        ),
        name="step",
    )(queries[0], keys[0], values[0], log_decay[0], w_out.reshape(16, DOUT), grad_out[0])
    mixed, qg, kg, vg, wg = pl.pallas_call(
        hand_out,
        out_shape=shapes,
        in_specs=[hbm] * 5,
        out_specs=(hbm,) * 5,
        scratch_shapes=[*(pltpu.VMEM(s.shape, s.dtype) for s in shapes), pltpu.SemaphoreType.DMA((2, 5))],
        compiler_params=pltpu.CompilerParams(vmem_limit_bytes=60 * 1024 * 1024),
        name="hand_out",
    )(*results)
    return mixed[None], qg[None], kg[None], vg[None], wg.reshape(2, HEADS, DOUT)


def solution(mesh):
    return jax.shard_map(
        shards,
        mesh=mesh,
        in_specs=(
            P("dp", "ctx", "head"),
            P("dp", "ctx", "head"),
            P("dp", "ctx", "head"),
            P("dp", "head", "ctx"),
            P(("ctx", "dp"), "head", None),
            P("dp", "ctx", None),
        ),
        out_specs=(
            P("dp", "ctx", "head"),
            P("dp", "ctx", "head"),
            P("dp", "ctx", "head"),
            P("dp", "ctx", "head"),
            P(("ctx", "dp"), "head", None),
        ),
        check_vma=False,
    )
```

```python
import jax
import jax.numpy as jnp
from jax import lax
from jax.experimental import pallas as pl
from jax.experimental.pallas import tpu as pltpu
from jax.sharding import PartitionSpec as P

DH = 128
BLOCK = 256
HEADS = 8
DOUT = 3072
HALF = DOUT // 2
CHIPS = 16
SCALE = 1.0 / DH
F32 = jnp.float32
BF16 = jnp.bfloat16
NT = (((1,), (1,)), ((), ()))
NN = (((1,), (0,)), ((), ()))
TN = (((0,), (0,)), ((), ()))


def mm(a, b, dims):
    return lax.dot_general(a, b, dims, preferred_element_type=F32)


class Ids:
    def __init__(self):
        self.names = {}

    def __call__(self, *name):
        return self.names.setdefault(name, len(self.names))


def kernel(
    q_in, k_in, v_in, ld_in, w_in, go_in,
    mixed_out, qg_out, kg_out, vg_out, wg_out,
    q_ref, k_ref, v_ref, ld_ref, go_ref, mixed_ref, qg_ref, kg_ref, vg_ref, wg_ref,
    panel, pt, cum, ccol, probs, intra, kpart, vpart, att, attp, gh,
    cf, sf, tf, rf, ef, inf, lowf, low, cb, sb, tb, rb, eb, inb, lowb, back,
    go_sib, att_t, att_sib,
    wp, xb, yb, wacc, wa, ya, xz,
    mp, macc, mr1, mr2,
    ssem, rsem, a2a_s, a2a_r, isem, osem,
):
    ctx, head, dp = lax.axis_index("ctx"), lax.axis_index("head"), lax.axis_index("dp")
    core, chip = ctx % 2, ctx // 2
    x, y = chip % 4, ctx // 8
    a = x * (1 - core) + y * core
    b = y * (1 - core) + x * core
    ap, am, ao = (a + 1) % 4, (a + 3) % 4, (a + 2) % 4
    bp, bm, bo = (b + 1) % 4, (b + 3) % 4, (b + 2) % 4
    z, zo = dp, 1 - dp

    def at(a1, b1):
        x1 = a1 * (1 - core) + b1 * core
        y1 = b1 * (1 - core) + a1 * core
        return ((y1 * 4 + x1) * 2 + core, head, dp)

    dev_ap, dev_am, dev_ao, dev_bp, dev_bm = at(ap, b), at(am, b), at(ao, b), at(a, bp), at(a, bm)
    dev_sib = (ctx + 1 - 2 * core, head, dp)
    dev_z = (ctx, head, zo)
    h1 = head + 1 - 2 * (head % 2)
    h2 = (head + 2) % 4
    h3 = (h1 + 2) % 4
    dev_h1, dev_h2 = (ctx, h1, dp), (ctx, h2, dp)

    ids = Ids()
    started = []

    def xfer(name, src, dst, dev):
        i = ids(*name)
        return pltpu.make_async_remote_copy(
            src_ref=src, dst_ref=dst, send_sem=ssem.at[i], recv_sem=rsem.at[i],
            device_id=dev, device_id_type=pl.DeviceIdType.MESH,
        )

    def send(name, src, dst, dev):
        copy = xfer(name, src, dst, dev)
        copy.start()
        started.append(copy)

    def recv(name, ref, dev):
        xfer(name, ref, ref, dev).wait_recv()

    def slot(a1, b1, z1):
        return core * 32 + z1 * 16 + b1 * 4 + a1

    mine = slot(a, b, z)
    pairs = ((w_in, panel.at[mine]), (ld_in, ld_ref), (k_in, k_ref), (v_in, v_ref), (q_in, q_ref), (go_in, go_ref))
    loads = [pltpu.make_async_copy(src, dst, isem.at[i]) for i, (src, dst) in enumerate(pairs)]
    for load in loads:
        load.start()

    barrier = pltpu.get_barrier_semaphore()

    def greet(i, carry):
        pl.semaphore_signal(
            barrier, inc=1, device_id=((chip + i) % CHIPS * 2 + core, head, dp), device_id_type=pl.DeviceIdType.MESH
        )
        return carry

    lax.fori_loop(1, CHIPS, greet, 0)
    for dev in (dev_sib, dev_z, dev_h1, dev_h2):
        pl.semaphore_signal(barrier, inc=1, device_id=dev, device_id_type=pl.DeviceIdType.MESH)
    for load in loads[1:4]:
        load.wait()

    t_row = lax.broadcasted_iota(jnp.int32, (BLOCK, BLOCK), 0)
    t_col = lax.broadcasted_iota(jnp.int32, (BLOCK, BLOCK), 1)
    upper = (t_row <= t_col).astype(F32)
    cum[...] = jnp.dot(ld_ref[...], upper, precision=lax.Precision.HIGHEST, preferred_element_type=F32)

    def heads(first, last, body):
        lax.fori_loop(first, last, body, 0, unroll=2 if (last - first) % 2 == 0 else 1)

    def lanes(h):
        return pl.ds(pl.multiple_of(h * DH, DH), DH)

    def pieces(buf, h, total, decay):
        for r in range(4):
            buf[h * 4 + r, 0:32, :] = total[r * 32 : (r + 1) * 32]
            buf[h * 4 + r, 32:40, :] = jnp.broadcast_to(decay, (8, DH))

    def fwd_share(h, carry):
        wide = jnp.broadcast_to(cum[pl.ds(h, 1), :], (DH, BLOCK))
        col = wide.T
        ccol[h] = col
        last = col[BLOCK - 1 : BLOCK, :]
        kw = (k_ref[:, lanes(h)].astype(F32) * jnp.exp(last - col)).astype(BF16)
        pieces(cf, h, mm(kw, v_ref[:, lanes(h)], TN), jnp.exp(last))
        return carry

    heads(0, 4, fwd_share)
    pl.semaphore_wait(barrier, CHIPS - 1 + 4)

    def whole(s):
        return panel.at[s]

    def part(s, h):
        return panel.at[s, :, pl.ds(h * HALF, HALF)]

    a_of = {0: a, 1: am, 2: ap, 3: ao}

    def b_sends(zi, k):
        zz = (z, zo)[zi]
        ref = whole(slot(a_of[k], b, zz))
        send(("bp", zi, k), ref, ref, dev_bp)
        send(("bm", zi, k), ref, ref, dev_bm)

    def a_sends(zi):
        ref = whole(slot(a, b, (z, zo)[zi]))
        send(("ap", zi), ref, ref, dev_ap)
        send(("am", zi), ref, ref, dev_am)
        send(("ao", zi), ref, ref, dev_ao)

    def step_a(zi):
        zz = (z, zo)[zi]
        left, right = slot(am, b, zz), slot(ap, b, zz)
        recv(("ap", zi), whole(left), dev_am)
        b_sends(zi, 1)
        recv(("am", zi), whole(right), dev_ap)
        b_sends(zi, 2)

    def step_ao(zi):
        far = slot(ao, b, (z, zo)[zi])
        recv(("ao", zi), whole(far), dev_ao)
        b_sends(zi, 3)
        sib_send(zi, 0)

    def step_b(zi, k):
        zz = (z, zo)[zi]
        below, above = slot(a_of[k], bm, zz), slot(a_of[k], bp, zz)
        recv(("bp", zi, k), whole(below), dev_bm)
        send(("bfp", zi, k), part(below, 0), part(below, 0), dev_bp)
        recv(("bm", zi, k), whole(above), dev_bp)
        send(("bfm", zi, k), part(above, 1), part(above, 1), dev_bm)

    def step_bo(zi, k):
        far = slot(a_of[k], bo, (z, zo)[zi])
        recv(("bfp", zi, k), part(far, 0), dev_bm)
        recv(("bfm", zi, k), part(far, 1), dev_bp)

    def step_z():
        recv(("z",), whole(slot(a, b, zo)), dev_z)
        a_sends(1)
        b_sends(1, 0)

    def row(c1, b1, z1):
        return panel.at[pl.ds(c1 * 32 + z1 * 16 + b1 * 4, 4)]

    def sib_send(zi, k):
        ref = row(core, (b, bm, bp, bo)[k], (z, zo)[zi])
        send(("sib", zi, k), ref, ref, dev_sib)

    def sib_recv(zi, k):
        recv(("sib", zi, k), row(1 - core, (a, am, ap, ao)[k], (z, zo)[zi]), dev_sib)

    loads[0].wait()
    send(("z",), whole(mine), whole(mine), dev_z)
    a_sends(0)
    b_sends(0, 0)
    def weights(h):
        col = ccol[h]
        spread = jnp.concatenate([col, col], axis=1) - cum[pl.ds(h, 1), :]
        rows = lax.broadcasted_iota(jnp.int32, (BLOCK, BLOCK), 0)
        cols = lax.broadcasted_iota(jnp.int32, (BLOCK, BLOCK), 1)
        return jnp.exp(jnp.where(rows >= cols, spread, -jnp.inf))

    def halves(own, sib, j, first):
        p, o = own[core * CHIPS + j], sib[j]
        return jnp.where(core == first, p, o), jnp.where(core == first, o, p)

    def own_half(buf):
        return buf.at[pl.ds(core * CHIPS, CHIPS)]

    def other_half(buf):
        return buf.at[pl.ds((1 - core) * CHIPS, CHIPS)]

    def merge(own, sib, out, first):
        def go(j, carry):
            p, s = halves(own, sib, j, first)
            out[j, 0:32, :] = (s[32:33] * p[0:32] + s[0:32]).astype(BF16)
            decay = s[32:40] * p[32:40]
            decay = jnp.concatenate([decay, decay], axis=0)
            top = decay.astype(BF16).astype(F32)
            mid = (decay - top).astype(BF16).astype(F32)
            place = lax.broadcasted_iota(jnp.int32, (16, DH), 0)
            three = jnp.where(place < 5, top, jnp.where(place < 10, mid, decay - top - mid))
            out[j, 32:48, :] = three.astype(BF16)
            return carry

        lax.fori_loop(0, CHIPS, go, 0, unroll=2)

    def split(own, sib, got, out, out_sib, first):
        def go(j, carry):
            p, _ = halves(own, sib, j, first)
            early = got[j].astype(F32)
            late = p[32:33] * early + p[0:32]
            out[core * CHIPS + j] = jnp.where(core == first, early, late).astype(BF16)
            out_sib[j] = jnp.where(core == first, late, early).astype(BF16)
            return carry

        lax.fori_loop(0, CHIPS, go, 0, unroll=2)

    def a2a(n, src, dst, i, out):
        other = (chip + i) % CHIPS if out else (chip + CHIPS - i) % CHIPS
        return pltpu.make_async_remote_copy(
            src_ref=src.at[other], dst_ref=dst.at[chip if out else other],
            send_sem=a2a_s.at[n, i], recv_sem=a2a_r.at[n, i],
            device_id=(other * 2 + core, head, dp), device_id_type=pl.DeviceIdType.MESH,
        )

    def a2a_start(n, src, dst):
        def go(i, carry):
            a2a(n, src, dst, i, True).start()
            return carry

        lax.fori_loop(1, CHIPS, go, 0)
        dst[chip] = src[chip]

    def a2a_recv(n, src, dst):
        def go(i, carry):
            a2a(n, src, dst, i, False).wait_recv()
            return carry

        lax.fori_loop(1, CHIPS, go, 0)

    def a2a_sent(n, src, dst):
        def go(i, carry):
            a2a(n, src, dst, i, True).wait_send()
            return carry

        lax.fori_loop(1, CHIPS, go, 0)

    def scan(got, out, reverse):
        def go(i, state):
            at_chip = CHIPS - 1 - i if reverse else i
            out[at_chip] = state.astype(BF16)
            three = got[at_chip, 32:48, :].astype(F32)
            decay = three[0:1] + three[5:6] + three[10:11]
            return state * decay + got[at_chip, 0:32, :].astype(F32)

        lax.fori_loop(0, CHIPS, go, jnp.zeros((32, DH), F32), unroll=2)

    def state_of(buf, h):
        return buf[pl.ds(h * 4, 4)].reshape(DH, DH)

    heads(4, HEADS, fwd_share)
    send(("f", 0), other_half(cf), sf, dev_sib)
    step_a(0)
    recv(("f", 0), sf, dev_sib)
    merge(cf, sf, tf, 0)
    a2a_start(0, tf, rf)
    loads[4].wait()
    loads[5].wait()
    send(("go",), go_ref, go_sib, dev_sib)

    def inside(h, carry):
        scores = mm(q_ref[:, lanes(h)], k_ref[:, lanes(h)], NT)
        p = (scores * SCALE * weights(h)).astype(BF16)
        probs[h] = p
        intra[:, lanes(h)] = mm(p, v_ref[:, lanes(h)], NN)
        return carry

    heads(0, 2, inside)
    step_ao(0)
    step_z()
    step_b(0, 0)
    heads(2, 4, inside)
    step_b(0, 1)
    step_b(0, 2)
    a2a_recv(0, tf, rf)
    scan(rf, ef, False)
    a2a_start(1, ef, inf)
    step_a(1)
    heads(4, HEADS, inside)
    step_b(0, 3)
    sib_send(0, 1)
    sib_send(0, 2)
    step_ao(1)
    step_b(1, 0)

    a2a_recv(1, ef, inf)
    split(cf, sf, inf, low, lowf, 0)
    send(("f", 1), lowf, own_half(low), dev_sib)

    r = lax.broadcasted_iota(jnp.int32, (1024, DH), 0)
    place = r >> 4
    pc, pz, pb, pa = place >> 5, (place >> 4) & 1, (place >> 2) & 3, place & 3
    px = jnp.where(pc == 0, pa, pb)
    py = jnp.where(pc == 0, pb, pa)
    feature = 2 * ((((py * 4) + px) * 2 + pc) * 2 + pz) + ((r >> 3) & 1)
    lane = lax.broadcasted_iota(jnp.int32, (1024, DH), 1)
    same = feature == lane
    for h in range(HEADS):
        pt[:, h * DH : (h + 1) * DH] = jnp.where(same & ((r & 7) == h), 1.0, 0.0).astype(BF16)

    step_b(1, 1)
    step_b(1, 2)
    recv(("f", 1), other_half(low), dev_sib)

    def attend(h, carry):
        inter = mm(q_ref[:, lanes(h)], state_of(low, h), NN)
        factor = SCALE * jnp.exp(ccol[h])
        att[:, lanes(h)] = (intra[:, lanes(h)] + inter * factor).astype(BF16)
        return carry

    heads(0, HEADS, attend)
    step_b(1, 3)
    sib_send(1, 1)
    sib_send(1, 2)

    def turn(i, carry):
        rows = pl.ds(pl.multiple_of(i * 256, 256), 256)
        att_t[rows, :] = mm(pt[rows, :], att[...], NT).astype(BF16)
        attp[:, rows] = mm(att[...], pt[rows, :], NT).astype(BF16)
        return carry

    lax.fori_loop(0, 4, turn, 0, unroll=2)
    other_rows = pl.ds(pl.multiple_of((1 - core) * 512, 512), 512)
    send(("att",), att_t.at[other_rows], att_sib, dev_sib)
    for k in range(4):
        step_bo(0, k)
    sib_send(0, 3)

    recv(("go",), go_sib, dev_sib)
    recv(("att",), att_sib, dev_sib)
    lo, hi = pl.ds(0, HALF), pl.ds(HALF, HALF)

    def widen(ref):
        return ref.astype(F32)

    def rows_b(b1):
        return pl.ds(pl.multiple_of(b1 * 64, 64), 64)

    def rows_a(a1):
        return pl.ds(pl.multiple_of(a1 * 16, 16), 16)

    def w_block(zi):
        zz = (zo, z)[zi]
        own = pl.ds(pl.multiple_of(core * 512 + zz * 256, 256), 256)
        sib = pl.ds(pl.multiple_of(zz * 256, 256), 256)

        def go(n, carry):
            cols = pl.ds(pl.multiple_of(n * 256, 256), 256)
            value = mm(att_t[own, :], go_ref[:, cols], NN) + mm(att_sib[sib, :], go_sib[:, cols], NN)
            wp[zi, :, cols] = value.astype(BF16)
            return carry

        lax.fori_loop(0, 12, go, 0, unroll=2)

    def w_first(zi):
        w_block(zi)
        send(("w", zi, 0), wp.at[zi, rows_b(bo), lo], xb.at[zi, 0], dev_bp)
        send(("w", zi, 1), wp.at[zi, rows_b(bo), hi], xb.at[zi, 1], dev_bm)
        send(("w", zi, 2), wp.at[zi, rows_b(bp), hi], yb.at[zi, 0, :, hi], dev_bp)
        send(("w", zi, 3), wp.at[zi, rows_b(bm), lo], yb.at[zi, 1, :, lo], dev_bm)

    def w_relay(zi):
        recv(("w", zi, 0), xb.at[zi, 0], dev_bm)
        wp[zi, rows_b(bp), lo] = (widen(wp[zi, rows_b(bp), lo]) + widen(xb[zi, 0])).astype(BF16)
        send(("w", zi, 4), wp.at[zi, rows_b(bp), lo], yb.at[zi, 0, :, lo], dev_bp)
        recv(("w", zi, 1), xb.at[zi, 1], dev_bp)
        wp[zi, rows_b(bm), hi] = (widen(wp[zi, rows_b(bm), hi]) + widen(xb[zi, 1])).astype(BF16)
        send(("w", zi, 5), wp.at[zi, rows_b(bm), hi], yb.at[zi, 1, :, hi], dev_bm)

    def v_first(zi):
        recv(("w", zi, 2), yb.at[zi, 0, :, hi], dev_bm)
        recv(("w", zi, 3), yb.at[zi, 1, :, lo], dev_bp)
        recv(("w", zi, 4), yb.at[zi, 0, :, lo], dev_bm)
        recv(("w", zi, 5), yb.at[zi, 1, :, hi], dev_bp)

        def go(n, carry):
            cols = pl.ds(pl.multiple_of(n * 256, 256), 256)
            total = widen(wp[zi, rows_b(b), cols]) + widen(yb[zi, 0, :, cols]) + widen(yb[zi, 1, :, cols])
            wacc[zi, :, cols] = total
            wa[zi, :, cols] = total.astype(BF16)
            return carry

        lax.fori_loop(0, 12, go, 0, unroll=2)
        for n, (a1, dev) in enumerate(((ao, dev_ao), (ap, dev_ap), (am, dev_am))):
            send(("v", zi, n), wa.at[zi, rows_a(a1)], ya.at[zi, n], dev)

    def v_last(zi):
        for n, dev in enumerate((dev_ao, dev_am, dev_ap)):
            recv(("v", zi, n), ya.at[zi, n], dev)
        return wacc[zi, rows_a(a), :] + widen(ya[zi, 0]) + widen(ya[zi, 1]) + widen(ya[zi, 2])

    w_first(0)
    for k in range(4):
        step_bo(1, k)
    sib_send(1, 3)
    w_first(1)
    for zi in range(2):
        for k in range(4):
            sib_recv(zi, k)

    def mix(dest, store):
        def go(n, carry):
            cols = pl.ds(pl.multiple_of(dest * 768 + n * 256, 256), 256)
            w = panel[:, :, cols].reshape(1024, 256)
            store(pl.ds(pl.multiple_of(n * 256, 256), 256), mm(attp[...], w, NN))
            return carry

        lax.fori_loop(0, 3, go, 0, unroll=3)

    def store_at(dest):
        def store(cols, value):
            mp[dest, :, cols] = value.astype(BF16)

        return store

    def store_own(cols, value):
        macc[:, cols] = value

    mix(h3, store_at(h3))
    send(("m", 0), mp.at[h3], mr1.at[0], dev_h1)
    mix(h1, store_at(h1))
    send(("m", 1), mp.at[h1], mr1.at[1], dev_h1)

    def heads_grad(i, carry):
        rows = panel[pl.ds(i * 16, 16)].reshape(256, DOUT)
        cols = pl.ds(pl.multiple_of(i * 256, 256), 256)
        gh[:, cols] = mm(go_ref[...], rows, NT).astype(BF16)
        return carry

    lax.fori_loop(0, 4, heads_grad, 0, unroll=2)
    by_head = []
    for n in range(4):
        by_head.append(mm(gh[...], pt[:, n * 256 : (n + 1) * 256], NN).astype(BF16))
    for n in range(4):
        gh[:, n * 256 : (n + 1) * 256] = by_head[n]

    def bwd_share(h, carry):
        qw = (q_ref[:, lanes(h)].astype(F32) * (SCALE * jnp.exp(ccol[h]))).astype(BF16)
        last = ccol[h, BLOCK - 1 : BLOCK, :]
        pieces(cb, h, mm(qw, gh[:, lanes(h)], TN), jnp.exp(last))
        return carry

    heads(0, HEADS, bwd_share)
    send(("k", 0), other_half(cb), sb, dev_sib)
    w_relay(0)
    recv(("k", 0), sb, dev_sib)
    merge(cb, sb, tb, 1)
    a2a_start(2, tb, rb)
    w_relay(1)
    mix(h2, store_at(h2))

    def grads(h, carry):
        g, kk, vv, qq = gh[:, lanes(h)], k_ref[:, lanes(h)], v_ref[:, lanes(h)], q_ref[:, lanes(h)]
        dp_h = (mm(g, vv, NT) * SCALE * weights(h)).astype(BF16)
        factor = SCALE * jnp.exp(ccol[h])
        qg = mm(dp_h, kk, NN) + mm(g, state_of(low, h), NT) * factor
        qg_ref[:, lanes(h)] = qg.astype(BF16)
        kpart[:, lanes(h)] = mm(dp_h, qq, TN)
        vpart[:, lanes(h)] = mm(probs[h], g, TN)
        return carry

    heads(0, 2, grads)
    recv(("m", 0), mr1.at[0], dev_h1)
    mp[h2] = (widen(mp[h2]) + widen(mr1[0])).astype(BF16)
    send(("m", 2), mp.at[h2], mr2, dev_h2)
    v_first(0)
    a2a_recv(2, tb, rb)
    scan(rb, eb, True)
    a2a_start(3, eb, inb)
    heads(2, 4, grads)
    v_first(1)
    heads(4, HEADS, grads)
    wa[0, rows_a(a), :] = v_last(0).astype(BF16)
    send(("vz",), wa.at[0, rows_a(a)], xz, dev_z)

    a2a_recv(3, eb, inb)
    split(cb, sb, inb, back, lowb, 1)
    send(("k", 1), lowb, own_half(back), dev_sib)
    outs = [
        pltpu.make_async_copy(src, dst, osem.at[i])
        for i, (src, dst) in enumerate(
            ((qg_ref, qg_out), (kg_ref, kg_out), (vg_ref, vg_out), (mixed_ref, mixed_out), (wg_ref, wg_out))
        )
    ]
    outs[0].start()
    mix(head, store_own)
    recv(("k", 1), other_half(back), dev_sib)

    def finish(h, carry):
        col = ccol[h]
        tail = jnp.exp(col[BLOCK - 1 : BLOCK, :] - col)
        state = state_of(back, h)
        kg = kpart[:, lanes(h)] + tail * mm(v_ref[:, lanes(h)], state, NT)
        vg = vpart[:, lanes(h)] + tail * mm(k_ref[:, lanes(h)], state, NN)
        kg_ref[:, lanes(h)] = kg.astype(BF16)
        vg_ref[:, lanes(h)] = vg.astype(BF16)
        return carry

    heads(0, HEADS, finish)
    outs[1].start()
    outs[2].start()

    wg_ref[...] = v_last(1)
    recv(("vz",), xz, dev_z)
    wg_ref[...] += widen(xz[...])
    outs[4].start()

    recv(("m", 1), mr1.at[1], dev_h1)
    recv(("m", 2), mr2, dev_h2)
    mixed_ref[...] = (macc[...] + widen(mr1[1]) + widen(mr2[...])).astype(BF16)
    outs[3].start()

    for copy in started:
        copy.wait_send()
    for n, src, dst in ((0, tf, rf), (1, ef, inf), (2, tb, rb), (3, eb, inb)):
        a2a_sent(n, src, dst)
    for out in outs:
        out.wait()


def hand_out(*refs):
    n = len(refs) // 3
    given, out, held, sems = refs[:n], refs[n : 2 * n], refs[2 * n : 3 * n], refs[-1]
    first = [pltpu.make_async_copy(given[i], held[i], sems.at[0, i]) for i in range(n)]
    second = [pltpu.make_async_copy(held[i], out[i], sems.at[1, i]) for i in range(n)]
    for copy in first:
        copy.start()
    for i in range(n):
        first[i].wait()
        second[i].start()
    for copy in second:
        copy.wait()


def shards(queries, keys, values, log_decay, w_out, grad_out):
    hbm = pl.BlockSpec(memory_space=pl.ANY)
    length = queries.shape[1]
    features = HEADS * DH
    shapes = (
        jax.ShapeDtypeStruct((length, DOUT // 4), BF16),
        jax.ShapeDtypeStruct((length, features), BF16),
        jax.ShapeDtypeStruct((length, features), BF16),
        jax.ShapeDtypeStruct((length, features), BF16),
        jax.ShapeDtypeStruct((16, DOUT), F32),
    )
    whole = pltpu.VMEM((length, features), BF16)
    wide = pltpu.VMEM((length, features), F32)
    piece = pltpu.VMEM((CHIPS, 48, DH), BF16)
    state = pltpu.VMEM((CHIPS, 32, DH), BF16)
    scan = [
        pltpu.VMEM((2 * CHIPS, 40, DH), F32), pltpu.VMEM((CHIPS, 40, DH), F32), piece, piece,
        state, state, state, pltpu.VMEM((2 * CHIPS, 32, DH), BF16),
    ]

    results = pl.pallas_call(
        kernel,
        out_shape=shapes,
        in_specs=[hbm] * 6,
        out_specs=(hbm,) * 5,
        scratch_shapes=[
            whole,
            whole,
            whole,
            pltpu.VMEM((HEADS, BLOCK), F32),
            pltpu.VMEM((BLOCK, DOUT), BF16),
            pltpu.VMEM((BLOCK, DOUT // 4), BF16),
            whole,
            whole,
            whole,
            pltpu.VMEM((16, DOUT), F32),
            pltpu.VMEM((64, 16, DOUT), BF16),
            pltpu.VMEM((features, features), BF16),
            pltpu.VMEM((HEADS, BLOCK), F32),
            pltpu.VMEM((HEADS, BLOCK, DH), F32),
            pltpu.VMEM((HEADS, BLOCK, BLOCK), BF16),
            wide,
            wide,
            wide,
            whole,
            whole,
            whole,
            *scan,
            *scan,
            pltpu.VMEM((BLOCK, DOUT), BF16),
            pltpu.VMEM((features, BLOCK), BF16),
            pltpu.VMEM((512, BLOCK), BF16),
            pltpu.VMEM((2, 256, DOUT), BF16),
            pltpu.VMEM((2, 2, 64, HALF), BF16),
            pltpu.VMEM((2, 2, 64, DOUT), BF16),
            pltpu.VMEM((2, 64, DOUT), F32),
            pltpu.VMEM((2, 64, DOUT), BF16),
            pltpu.VMEM((2, 3, 16, DOUT), BF16),
            pltpu.VMEM((16, DOUT), BF16),
            pltpu.VMEM((4, BLOCK, 768), BF16),
            pltpu.VMEM((BLOCK, 768), F32),
            pltpu.VMEM((2, BLOCK, 768), BF16),
            pltpu.VMEM((BLOCK, 768), BF16),
            pltpu.SemaphoreType.DMA((88,)),
            pltpu.SemaphoreType.DMA((88,)),
            pltpu.SemaphoreType.DMA((4, CHIPS)),
            pltpu.SemaphoreType.DMA((4, CHIPS)),
            pltpu.SemaphoreType.DMA((6,)),
            pltpu.SemaphoreType.DMA((5,)),
        ],
        compiler_params=pltpu.CompilerParams(
            collective_id=0, has_side_effects=True, vmem_limit_bytes=60 * 1024 * 1024
        ),
        name="step",
    )(queries[0], keys[0], values[0], log_decay[0], w_out.reshape(16, DOUT), grad_out[0])
    mixed, qg, kg, vg, wg = pl.pallas_call(
        hand_out,
        out_shape=shapes,
        in_specs=[hbm] * 5,
        out_specs=(hbm,) * 5,
        scratch_shapes=[*(pltpu.VMEM(s.shape, s.dtype) for s in shapes), pltpu.SemaphoreType.DMA((2, 5))],
        compiler_params=pltpu.CompilerParams(vmem_limit_bytes=60 * 1024 * 1024),
        name="hand_out",
    )(*results)
    return mixed[None], qg[None], kg[None], vg[None], wg.reshape(2, HEADS, DOUT)


def solution(mesh):
    return jax.shard_map(
        shards,
        mesh=mesh,
        in_specs=(
            P("dp", "ctx", "head"),
            P("dp", "ctx", "head"),
            P("dp", "ctx", "head"),
            P("dp", "head", "ctx"),
            P(("ctx", "dp"), "head", None),
            P("dp", "ctx", None),
        ),
        out_specs=(
            P("dp", "ctx", "head"),
            P("dp", "ctx", "head"),
            P("dp", "ctx", "head"),
            P("dp", "ctx", "head"),
            P(("ctx", "dp"), "head", None),
        ),
        check_vma=False,
    )
```
